32 devices in a mesh: gx: 4 (over y, x), gy: 4 (over z), gz: 2 (over core).
Axes of the slice: x: 2, y: 2, z: 4, core: 2. Of those that a mesh axis runs over, the one named last changes fastest.
Arguments:
- velocity: float32 [3, 128, 128, 256], P(None, 'gx', 'gy', 'gz'), may hold values from -1100 to 1100
- view_sign: int32 [8], replicated, may hold values from 0 to 1
- transfer: float32 [8, 4, 128], replicated, may hold values from 0 to 1
Outputs:
- image: float32 [8, 4, 128, 256], P(None, None, 'gy', 'gz')
The draws below stay inside these ranges and needn't reach their ends.
All inputs are finite; a program needn't handle non-finite values.
Results may differ from the reference program's by a relative error of at most 0.0003.
Values sent between devices are 32-bit elements; how exact they have to be, the bound alone decides.
No kernel may reach another device: no remote copies, remote signals or barrier semaphores. Data moves between devices by JAX's collectives and lax.ppermute only.
A program may use at most 64 MiB of HBM per device.

```python
import math
import jax
import jax.numpy as jnp
from jax import lax

VIEWS = 8
BINS = 128
NX = 128
NY = 128
NZ = 256


def draw_velocity(key, part):
    keys = jax.random.split(key, 3)
    row_scale = jnp.exp(jax.random.uniform(keys[1], (1, 1, NY, 1), jnp.float32, 0.0, math.log(10.0)))
    col_scale = jnp.exp(jax.random.uniform(keys[2], (1, 1, 1, NZ), jnp.float32, 0.0, math.log(10.0)))
    row_place = jnp.arange(NY, dtype=jnp.float32).reshape(1, 1, NY, 1)
    rising = jnp.sqrt(1.0 + 2.0 * row_place / NY)
    base = jnp.clip(jax.random.normal(keys[0], (3, NX, NY, NZ), jnp.float32), -6.0, 6.0)
    return base * row_scale * col_scale * rising


def touch_ends(drawn, own_key, smallest, high):
    extent = drawn.shape
    spot = [jax.random.randint(jax.random.fold_in(own_key, axis), (), 0, extent[axis]) for axis in range(len(extent))]
    drawn = drawn.at[tuple(spot)].set(smallest)
    longest = extent.index(max(extent))
    spot[longest] = (spot[longest] + 1) % extent[longest]
    return drawn.at[tuple(spot)].set(high)


def setup_inputs(seed: int = 0) -> dict:
    key_of = jax.random.split(jax.random.key(seed), 4)
    return {
        "velocity": draw_velocity(jax.random.fold_in(key_of[3], 71), 0),
        "view_sign": touch_ends(jax.random.randint(key_of[1], (VIEWS,), 0, 2), jax.random.fold_in(key_of[1], 1), 0, 1).astype(jnp.int32),
        "transfer": jnp.clip(jax.random.uniform(key_of[2], (VIEWS, 4, BINS), jnp.float32, 0.0, 1.0), 0.0, 1.0),
    }


def q_criterion(padded):
    grad_x = (padded[:, 2:, 1:-1, 1:-1] - padded[:, :-2, 1:-1, 1:-1]) * 0.5
    grad_y = (padded[:, 1:-1, 2:, 1:-1] - padded[:, 1:-1, :-2, 1:-1]) * 0.5
    grad_z = (padded[:, 1:-1, 1:-1, 2:] - padded[:, 1:-1, 1:-1, :-2]) * 0.5
    gradients = (grad_x, grad_y, grad_z)
    summed = jnp.zeros(grad_x.shape[1:], jnp.float32)
    for outer in range(3):
        for inner in range(3):
            summed = summed + gradients[inner][outer] * gradients[outer][inner]
    return -0.5 * summed


def reference(velocity, view_sign, transfer):
    padded = jnp.pad(velocity, ((0, 0), (1, 1), (1, 1), (1, 1)))
    energy = jnp.sum(velocity * velocity) / (NX * NY * NZ)
    colour_table = transfer.reshape(VIEWS * 4, BINS)
    bin_levels = jnp.arange(BINS, dtype=jnp.float32)[:, None]
    ascending = (view_sign == 0)[:, None, None, None]

    def march_step(marched, depth_index):
        front_colour, optical_sum, back_colour = marched
        window = lax.dynamic_slice_in_dim(padded, depth_index.astype(jnp.int32), 3, 1)
        qcrit = q_criterion(window)[0]
        bin_coord = (BINS - 1) * jax.nn.sigmoid(2.0 * qcrit / (energy + 1e-6))
        hat_weights = jnp.maximum(0.0, 1.0 - jnp.abs(bin_coord.reshape(1, -1) - bin_levels))
        looked = jnp.dot(colour_table, hat_weights, precision=lax.Precision.HIGHEST,
                         preferred_element_type=jnp.float32).reshape(VIEWS, 4, NY, NZ)
        optical = 3.0 * looked[:, 3:4] / NX
        colour = looked[:, 0:3]
        absorbed = 1.0 - jnp.exp(-optical)
        front_colour = front_colour + jnp.exp(-optical_sum) * absorbed * colour
        back_colour = absorbed * colour + jnp.exp(-optical) * back_colour
        optical_sum = optical_sum + optical
        return (front_colour, optical_sum, back_colour), None

    start = (jnp.zeros((VIEWS, 3, NY, NZ), jnp.float32),
             jnp.zeros((VIEWS, 1, NY, NZ), jnp.float32),
             jnp.zeros((VIEWS, 3, NY, NZ), jnp.float32))
    marched, _ = lax.scan(march_step, start, jnp.arange(NX, dtype=jnp.int32))
    front_colour, optical_sum, back_colour = marched
    tinted = jnp.where(ascending, front_colour, back_colour)
    opacity = 1.0 - jnp.exp(-optical_sum)
    return jnp.concatenate([tinted, opacity], axis=1)
```

```python
import functools
import math

import jax
import jax.numpy as jnp
from jax import lax
from jax.experimental import pallas as pl
from jax.experimental.pallas import tpu as pltpu
from jax.sharding import PartitionSpec as P

SUB, LANES = 8, 128
AXES = ("gx", "gy", "gz")
ANY = pl.BlockSpec(memory_space=pl.ANY)
VMEM = pl.BlockSpec(memory_space=pltpu.VMEM)
SMEM = pl.BlockSpec(memory_space=pltpu.SMEM)
f32 = jnp.float32


def swap(x, axis, bit_mask):
    n = lax.axis_size(axis)
    return lax.ppermute(x, axis, [(i, i ^ bit_mask) for i in range(n)])


def swap_across(x, axis):
    n = lax.axis_size(axis)
    return lax.ppermute(x, axis, [(i, (i + 1) % n if i % 2 else (i - 1) % n) for i in range(n)])


def flags(sizes):
    out = []
    for axis, n in zip(AXES, sizes):
        i = lax.axis_index(axis)
        out.append((lax.rem(i, 2) == 0, i == 0, i == n - 1))
    return out


def faces_kernel(sizes, v_ref, *outs):
    comps, depth, rows, cols = v_ref.shape
    tiles = rows // SUB
    (ex, _, _), (ey, _, _), (ez, _, _) = flags(sizes)
    outs = list(outs)
    sq_ref = outs.pop()
    groups = depth * tiles // LANES
    lane = lax.broadcasted_iota(jnp.int32, (SUB, LANES), 1)
    zouts = []
    for axis, even, extent in (("x", ex, depth), ("y", ey, rows), ("z", ez, cols)):
        n = sizes["xyz".index(axis)]
        for far in range(0 if n == 1 else 1 if n == 2 else 2):
            out = outs.pop(0)
            at = jnp.where(even, extent - 1, 0)
            if far:
                at = extent - 1 - at
            if axis == "x":
                for c in range(comps):
                    out[c] = v_ref[c, at]
            elif axis == "y":
                for c in range(comps):
                    for x in range(depth):
                        out[c, pl.ds(x, 1), :] = v_ref[c, x, pl.ds(at, 1), :]
            else:
                zouts.append((out, at))
    per = LANES // tiles
    for g in range(groups):

        def body(i, carry):
            squares, picked = carry
            x = g * per + i
            picked = list(picked)
            for c in range(comps):
                for j in range(tiles):
                    tile = v_ref[c, x, pl.ds(j * SUB, SUB), :]
                    squares = squares + tile * tile
                    to = i * tiles + j
                    for o, (_, at) in enumerate(zouts):
                        moved = pltpu.roll(tile, lax.rem(to - at + cols, cols), 1)[:, :LANES]
                        picked[o * comps + c] = jnp.where(lane == to, moved, picked[o * comps + c])
            return squares, tuple(picked)

        zero = jnp.zeros((SUB, LANES), f32)
        squares = zero if g == 0 else sq_ref[...]
        squares, picked = lax.fori_loop(
            0, per, body, (squares, (zero,) * (comps * len(zouts))), unroll=4
        )
        sq_ref[...] = squares
        for o, (out, _) in enumerate(zouts):
            for c in range(comps):
                out[g, c] = picked[o * comps + c]


def q_kernel(sizes, v_hbm, *refs):
    comps, depth, rows, cols = v_hbm.shape
    tiles = rows // SUB
    nx = sizes[0]
    counts = [0 if n == 1 else 1 if n == 2 else 2 for n in sizes]
    halos = [[refs[sum(counts[:a]) + k] for k in range(counts[a])] for a in range(3)]
    refs = refs[sum(counts):]
    outs, (padded, zh, sem) = refs[:nx], refs[nx:]
    info = flags(sizes)
    copy = pltpu.make_async_copy(
        v_hbm, padded.at[:, pl.ds(1, depth), pl.ds(SUB, rows), :], sem.at[0]
    )
    copy.start()

    def both(axis, index):
        even, first, last = info[axis]
        if not halos[axis]:
            return None, None
        near = halos[axis][0][index]
        far = halos[axis][-1][index]
        low = jnp.where(first, 0.0, jnp.where(even, far, near))
        high = jnp.where(last, 0.0, jnp.where(even, near, far))
        return low, high

    for c in range(comps):
        low, high = both(0, c)
        shape = (rows, cols)
        padded[c, 0, pl.ds(SUB, rows), :] = jnp.zeros(shape, f32) if low is None else low
        padded[c, depth + 1, pl.ds(SUB, rows), :] = jnp.zeros(shape, f32) if high is None else high
        low, high = both(1, c)
        zero = jnp.zeros((1, cols), f32)
        for x in range(depth):
            padded[c, 1 + x, pl.ds(SUB - 1, 1), :] = zero if low is None else low[x:x + 1]
            padded[c, 1 + x, pl.ds(SUB + rows, 1), :] = zero if high is None else high[x:x + 1]
    groups = depth * tiles // LANES
    for g in range(groups):
        for c in range(comps):
            low, high = both(2, (g, c))
            zero = jnp.zeros((SUB, LANES), f32)
            zh[0, g, c] = zero if low is None else low
            zh[1, g, c] = zero if high is None else high
    lane = lax.broadcasted_iota(jnp.int32, (SUB, cols), 1)
    me = lax.axis_index("gx")
    piece_tiles = tiles // nx
    per = LANES // tiles
    copy.wait()
    for k in range(nx):
        for p in range(piece_tiles):
            j = jnp.bitwise_xor(me, k) * piece_tiles + p
            base = j * SUB + SUB
            for g in range(groups):
                zlow = [zh[0, g, c] for c in range(comps)]
                zhigh = [zh[1, g, c] for c in range(comps)]

                def body(i, carry):
                    x = g * per + i
                    at = i * tiles + j
                    dx, dy, dz = [], [], []
                    for c in range(comps):
                        here = padded[c, x + 1, pl.ds(pl.multiple_of(base, SUB), SUB), :]
                        dx.append(
                            padded[c, x + 2, pl.ds(pl.multiple_of(base, SUB), SUB), :]
                            - padded[c, x, pl.ds(pl.multiple_of(base, SUB), SUB), :]
                        )
                        dy.append(
                            padded[c, x + 1, pl.ds(base + 1, SUB), :]
                            - padded[c, x + 1, pl.ds(base - 1, SUB), :]
                        )
                        lo = pltpu.roll(zlow[c], lax.rem(cols - at, cols), 1)
                        hi = pltpu.roll(zhigh[c], cols - 1 - at, 1)
                        up = jnp.where(lane == cols - 1, hi, pltpu.roll(here, cols - 1, 1))
                        down = jnp.where(lane == 0, lo, pltpu.roll(here, 1, 1))
                        dz.append(up - down)
                    cross = dy[0] * dx[1] + dz[0] * dx[2] + dz[1] * dy[2]
                    total = dx[0] * dx[0] + dy[1] * dy[1] + dz[2] * dz[2] + (cross + cross)
                    outs[k][x, pl.ds(p * SUB, SUB), :] = total
                    return carry

                lax.fori_loop(0, per, body, 0, unroll=4)


def render_kernel(nx, cell_count, *refs):
    refs = list(refs)
    pieces = [refs.pop(0) for _ in range(nx)]
    sums = [refs.pop(0) for _ in range(nx)]
    sign_ref, table_ref, out_ref, low_ref, frac_ref, tab_ref = refs
    depth, rows, cols = pieces[0].shape
    bins = table_ref.shape[-1]
    views = sign_ref.shape[0]
    depth_total = depth * nx
    me = lax.axis_index("gx")
    squares = sums[0][...]
    for s in sums[1:]:
        squares = squares + s[...]
    energy = jnp.sum(squares, keepdims=True) / cell_count
    scale = -0.25 / (energy + 1e-06)
    scale = jnp.broadcast_to(scale, (SUB, cols))
    for k in range(nx):
        base = jnp.bitwise_xor(me, k) * depth

        def classify(x, carry):
            for p in range(rows // SUB):
                part = pieces[k][x, pl.ds(p * SUB, SUB), :] * scale
                coord = (bins - 1) / (1.0 + jnp.exp(-part))
                low = coord.astype(jnp.int32)
                low_ref[base + x, pl.ds(p * SUB, SUB), :] = low
                frac_ref[base + x, pl.ds(p * SUB, SUB), :] = coord - low.astype(f32)
            return carry

        lax.fori_loop(0, depth, classify, 0, unroll=8)

    table = table_ref[...]
    lane = lax.broadcasted_iota(jnp.int32, table.shape, 1)
    row = lax.broadcasted_iota(jnp.int32, table.shape, 0)
    factor = -3.0 / depth_total * math.log2(math.e)
    table = jnp.where(lax.rem(row, 4) == 3, table * factor, table)
    step = jnp.where(lane == bins - 1, 0.0, pltpu.roll(table, bins - 1, 1) - table)
    tab_ref[0] = table
    tab_ref[1] = step

    for p in range(rows // SUB):

        def view_body(v, carry):
            forward = sign_ref[v] == 0
            start = jnp.where(forward, 0, depth_total - 1)
            stride = jnp.where(forward, 1, -1)
            values = [
                jnp.broadcast_to(tab_ref[0, pl.ds(v * 4 + c, 1), :], (SUB, bins)) for c in range(4)
            ]
            steps = [
                jnp.broadcast_to(tab_ref[1, pl.ds(v * 4 + c, 1), :], (SUB, bins)) for c in range(4)
            ]

            def march(i, state):
                light, total, red, green, blue = state
                x = start + stride * i
                low = low_ref[x, pl.ds(p * SUB, SUB), :]
                frac = frac_ref[x, pl.ds(p * SUB, SUB), :]

                def look(c):
                    pick = functools.partial(
                        jnp.take_along_axis, indices=low, axis=1, mode="promise_in_bounds"
                    )
                    return pick(values[c]) + frac * pick(steps[c])

                exponent = look(3)
                through = jnp.exp2(exponent)
                weight = light * (1.0 - through)
                return (
                    light * through,
                    total + exponent,
                    red + weight * look(0),
                    green + weight * look(1),
                    blue + weight * look(2),
                )

            zero = jnp.zeros((SUB, cols), f32)
            _, total, red, green, blue = lax.fori_loop(
                0, depth_total, march, (jnp.ones((SUB, cols), f32), zero, zero, zero, zero), unroll=8
            )
            for c, value in enumerate((red, green, blue, 1.0 - jnp.exp2(total))):
                out_ref[v, c, pl.ds(p * SUB, SUB), :] = value
            return carry

        lax.fori_loop(0, views, view_body, 0)


def assemble_kernel(nx, *refs):
    pieces, out, sem = refs[:nx], refs[nx], refs[nx + 1]
    rows = pieces[0].shape[2]
    me = lax.axis_index("gx")
    copies = []
    for k in range(nx):
        at = pl.multiple_of(jnp.bitwise_xor(me, k) * rows, SUB)
        copies.append(pltpu.make_async_copy(pieces[k], out.at[:, :, pl.ds(at, rows), :], sem.at[k]))
        copies[-1].start()
    for copy in copies:
        copy.wait()


def on_device(velocity, view_sign, transfer):
    comps, depth, rows, cols = velocity.shape
    views, channels, bins = transfer.shape
    sizes = tuple(lax.axis_size(a) for a in AXES)
    nx = sizes[0]
    assert all(n & (n - 1) == 0 for n in sizes)
    assert cols == LANES and bins == LANES and rows % (SUB * nx) == 0
    assert depth * (rows // SUB) % LANES == 0
    cell_count = depth * rows * cols * math.prod(sizes)
    counts = [0 if n == 1 else 1 if n == 2 else 2 for n in sizes]
    groups = depth * (rows // SUB) // LANES
    face = [(comps, rows, cols), (comps, depth, cols), (groups, comps, SUB, LANES)]
    shapes = [jax.ShapeDtypeStruct(face[a], f32) for a in range(3) for _ in range(counts[a])]
    tile = jax.ShapeDtypeStruct((SUB, LANES), f32)
    *sent, squares = pl.pallas_call(
        functools.partial(faces_kernel, sizes),
        out_shape=shapes + [tile],
        in_specs=[VMEM],
        out_specs=[VMEM] * (len(shapes) + 1),
        name="faces",
    )(velocity)
    kinds = [(AXES[a], far) for a in range(3) for far in range(counts[a])]
    halos = [
        swap_across(x, axis) if far else swap(x, axis, 1) for x, (axis, far) in zip(sent, kinds)
    ]
    part_rows = rows // nx
    piece = jax.ShapeDtypeStruct((depth, part_rows, cols), f32)
    q_pieces = pl.pallas_call(
        functools.partial(q_kernel, sizes),
        out_shape=[piece] * nx,
        in_specs=[ANY] + [VMEM] * len(halos),
        out_specs=[VMEM] * nx,
        scratch_shapes=[
            pltpu.VMEM((comps, depth + 2, rows + 2 * SUB, cols), f32),
            pltpu.VMEM((2, groups, comps, SUB, LANES), f32),
            pltpu.SemaphoreType.DMA((1,)),
        ],
        name="q",
    )(velocity, *halos)
    for axis in ("gz", "gy"):
        for bit in range(lax.axis_size(axis).bit_length() - 1):
            squares = squares + swap(squares, axis, 1 << bit)
    order = sorted(range(1, nx), key=lambda k: -k)
    got = {0: q_pieces[0]}
    for k in order:
        got[k] = swap(q_pieces[k], "gx", k)
    sums = [squares] + [swap(squares, "gx", k) for k in range(1, nx)]
    image_piece = pl.pallas_call(
        functools.partial(render_kernel, nx, cell_count),
        out_shape=jax.ShapeDtypeStruct((views, channels, part_rows, cols), f32),
        in_specs=[VMEM] * (2 * nx) + [SMEM, VMEM],
        out_specs=VMEM,
        scratch_shapes=[
            pltpu.VMEM((depth * nx, part_rows, cols), jnp.int32),
            pltpu.VMEM((depth * nx, part_rows, cols), f32),
            pltpu.VMEM((2, views * channels, bins), f32),
        ],
        name="render",
    )(*[got[k] for k in range(nx)], *sums, view_sign, transfer.reshape(views * channels, bins))
    images = {0: image_piece}
    for k in order:
        images[k] = swap(image_piece, "gx", k)
    return pl.pallas_call(
        functools.partial(assemble_kernel, nx),
        out_shape=jax.ShapeDtypeStruct((views, channels, rows, cols), f32),
        in_specs=[VMEM] * nx,
        out_specs=ANY,
        scratch_shapes=[pltpu.SemaphoreType.DMA((nx,))],
        name="assemble",
    )(*[images[k] for k in range(nx)])


def solution(mesh):
    in_specs = (P(None, "gx", "gy", "gz"), P(), P())
    out_specs = P(None, None, "gy", "gz")
    return jax.shard_map(
        on_device, mesh=mesh, in_specs=in_specs, out_specs=out_specs, check_vma=False
    )
```

```python
import functools
import math

import jax
import jax.numpy as jnp
from jax import lax
from jax.experimental import pallas as pl
from jax.experimental.pallas import tpu as pltpu
from jax.sharding import PartitionSpec as P

SUB, LANES = 8, 128
AXES = ("gx", "gy", "gz")
ANY = pl.BlockSpec(memory_space=pl.ANY)
VMEM = pl.BlockSpec(memory_space=pltpu.VMEM)
SMEM = pl.BlockSpec(memory_space=pltpu.SMEM)
f32 = jnp.float32
MARCH_UNROLL = 32
CHUNKS = 4


def limit(mib):
    return pltpu.CompilerParams(vmem_limit_bytes=mib * 2**20)


def swap(x, axis, bit_mask):
    n = lax.axis_size(axis)
    return lax.ppermute(x, axis, [(i, i ^ bit_mask) for i in range(n)])


def swap_across(x, axis):
    n = lax.axis_size(axis)
    return lax.ppermute(x, axis, [(i, (i + 1) % n if i % 2 else (i - 1) % n) for i in range(n)])


def flags(sizes):
    out = []
    for axis, n in zip(AXES, sizes):
        i = lax.axis_index(axis)
        out.append((lax.rem(i, 2) == 0, i == 0, i == n - 1))
    return out


def lookup(table, index):
    numbers = lax.GatherDimensionNumbers(
        offset_dims=(),
        collapsed_slice_dims=(1,),
        start_index_map=(1,),
        operand_batching_dims=(0,),
        start_indices_batching_dims=(0,),
    )
    return lax.gather(
        table, index[..., None], numbers, (1, 1), mode=lax.GatherScatterMode.PROMISE_IN_BOUNDS
    )


def faces_kernel(sizes, counts, v_hbm, *refs):
    comps, depth, rows, cols = v_hbm.shape
    tiles = rows // SUB
    info = flags(sizes)
    refs = list(refs)
    x_refs = [refs.pop(0) for _ in range(counts[0])]
    y_refs = [refs.pop(0) for _ in range(counts[1])]
    z_refs = [refs.pop(0) for _ in range(counts[2])]
    sq_ref, v_ref, sem = refs
    chunk = depth // CHUNKS
    copies = []
    for n in range(CHUNKS):
        part = pl.ds(n * chunk, chunk)
        copies.append(pltpu.make_async_copy(v_hbm.at[:, part], v_ref.at[:, part], sem.at[n]))
        copies[-1].start()

    def edge(axis, far, extent):
        at = jnp.where(info[axis][0], extent - 1, 0)
        return extent - 1 - at if far else at

    lane = lax.broadcasted_iota(jnp.int32, (SUB, LANES), 1)
    groups = depth * tiles // LANES
    zero = jnp.zeros((SUB, LANES), f32)
    picked = [[[zero] * comps for _ in range(groups)] for _ in z_refs]
    squares = [zero] * 4
    for n in range(CHUNKS):
        copies[n].wait()
        for x in range(n * chunk, (n + 1) * chunk):
            for far, out in enumerate(y_refs):
                at = edge(1, far, rows)
                for c in range(comps):
                    out[c, pl.ds(x, 1), :] = v_ref[c, x, pl.ds(at, 1), :]
            for c in range(comps):
                for j in range(tiles):
                    tile = v_ref[c, x, pl.ds(j * SUB, SUB), :]
                    squares[j % 4] = squares[j % 4] + tile * tile
                    group, to = divmod(x * tiles + j, LANES)
                    for far in range(len(z_refs)):
                        at = edge(2, far, cols)
                        moved = pltpu.roll(tile, lax.rem(to - at + cols, cols), 1)
                        old = picked[far][group][c]
                        picked[far][group][c] = jnp.where(lane == to, moved, old)
    for far, out in enumerate(x_refs):
        for c in range(comps):
            out[c] = v_ref[c, edge(0, far, depth)]
    total = (squares[0] + squares[1]) + (squares[2] + squares[3])
    sq_ref[...] = total
    for far, out in enumerate(z_refs):
        for g in range(groups):
            for c in range(comps):
                out[g * comps + c] = picked[far][g][c]
        out[groups * comps] = total


def attach_kernel(faces, tiles, *refs):
    face_refs, tile_refs = refs[:faces], refs[faces : faces + tiles]
    outs, sum_ref = refs[faces + tiles : -1], refs[-1]
    total = tile_refs[0][...]
    for t in tile_refs[1:]:
        total = total + t[...]
    sum_ref[...] = total
    for face, out in zip(face_refs, outs):
        comps = face.shape[0]
        out[pl.ds(0, comps)] = face[...]
        out[comps, pl.ds(0, SUB), :] = total


def q_kernel(sizes, counts, attached, extras, v_hbm, *refs):
    comps, depth, rows, cols = v_hbm.shape
    tiles = rows // SUB
    nx = sizes[0]
    refs = list(refs)
    halos = [[refs.pop(0) for _ in range(counts[a])] for a in range(3)]
    extra = [refs.pop(0) for _ in range(extras)]
    outs, (padded, sem) = refs[:nx], refs[nx:]
    info = flags(sizes)
    copy = pltpu.make_async_copy(
        v_hbm, padded.at[:, pl.ds(1, depth), pl.ds(SUB, rows), :], sem.at[0]
    )
    copy.start()

    def both(axis, index):
        even, first, last = info[axis]
        if not halos[axis]:
            return 0.0, 0.0
        near = halos[axis][0][index]
        far = halos[axis][-1][index]
        low = jnp.where(first, 0.0, jnp.where(even, far, near))
        high = jnp.where(last, 0.0, jnp.where(even, near, far))
        return low, high

    for c in range(comps):
        for end, value in zip((0, depth + 1), both(0, c)):
            padded[c, end, pl.ds(SUB, rows), :] = jnp.broadcast_to(value, (rows, cols))
        for end, value in zip((SUB - 1, SUB + rows), both(1, c)):
            value = jnp.broadcast_to(value, (depth, cols))
            for x in range(depth):
                padded[c, 1 + x, pl.ds(end, 1), :] = value[x : x + 1]
    tile_sum = extra[0][...]
    for t in extra[1:]:
        tile_sum = tile_sum + t[...]
    for near_far in halos[1][:attached]:
        tile_sum = tile_sum + near_far[comps, pl.ds(0, SUB), :]
    for out in outs:
        out[depth, pl.ds(0, SUB), :] = tile_sum
    groups = depth * tiles // LANES
    lane = lax.broadcasted_iota(jnp.int32, (SUB, cols), 1)
    me = lax.axis_index("gx")
    piece_tiles = tiles // nx
    per = LANES // tiles
    zeven = info[2][0]
    zero = jnp.zeros((SUB, LANES), f32)
    zhalo = []
    for g in range(groups):
        zhalo.append([])
        for c in range(comps):
            if counts[2] == 1:
                zhalo[g].append(halos[2][0][g * comps + c])
            else:
                zhalo[g].append([zero + h for h in both(2, g * comps + c)])
    copy.wait()
    for k in range(nx):
        for p in range(piece_tiles):
            j = jnp.bitwise_xor(me, k) * piece_tiles + p
            base = j * SUB + SUB
            middle = pl.ds(pl.multiple_of(base, SUB), SUB)
            for x in range(depth):
                g, i = divmod(x, per)
                at = i * tiles + j
                dx, dy, dz = [], [], []
                for c in range(comps):
                    here = padded[c, x + 1, middle, :]
                    dx.append(padded[c, x + 2, middle, :] - padded[c, x, middle, :])
                    dy.append(
                        padded[c, x + 1, pl.ds(base + 1, SUB), :]
                        - padded[c, x + 1, pl.ds(base - 1, SUB), :]
                    )
                    if counts[2] == 1:
                        shift = jnp.where(zeven, cols - 1 - at, lax.rem(cols - at, cols))
                        moved = pltpu.roll(zhalo[g][c], shift, 1)
                        high = jnp.where(zeven, moved, 0.0)
                        low = jnp.where(zeven, 0.0, moved)
                    else:
                        low = pltpu.roll(zhalo[g][c][0], lax.rem(cols - at, cols), 1)
                        high = pltpu.roll(zhalo[g][c][1], cols - 1 - at, 1)
                    up = jnp.where(lane == cols - 1, high, pltpu.roll(here, cols - 1, 1))
                    down = jnp.where(lane == 0, low, pltpu.roll(here, 1, 1))
                    dz.append(up - down)
                cross = dy[0] * dx[1] + dz[0] * dx[2] + dz[1] * dy[2]
                total = dx[0] * dx[0] + dy[1] * dy[1] + dz[2] * dz[2] + (cross + cross)
                outs[k][x, pl.ds(p * SUB, SUB), :] = total


def render_kernel(nx, cell_count, *refs):
    refs = list(refs)
    pieces = [refs.pop(0) for _ in range(nx)]
    sign_ref, table_ref, out_ref, low_ref, frac_ref, tab_ref = refs
    planes, rows, cols = pieces[0].shape
    depth = planes - 1
    bins = table_ref.shape[-1]
    views = sign_ref.shape[0]
    depth_total = depth * nx
    me = lax.axis_index("gx")
    squares = pieces[0][depth, pl.ds(0, SUB), :]
    for piece in pieces[1:]:
        squares = squares + piece[depth, pl.ds(0, SUB), :]
    energy = jnp.sum(squares, keepdims=True) / cell_count
    scale = -0.25 / (energy + 1e-06)
    scale = jnp.broadcast_to(scale, (SUB, cols))
    for k in range(nx):
        base = jnp.bitwise_xor(me, k) * depth

        def classify(x, carry):
            for p in range(rows // SUB):
                part = pieces[k][x, pl.ds(p * SUB, SUB), :] * scale
                coord = (bins - 1) / (1.0 + jnp.exp(-part))
                low = coord.astype(jnp.int32)
                low_ref[base + x, pl.ds(p * SUB, SUB), :] = low
                frac_ref[base + x, pl.ds(p * SUB, SUB), :] = coord - low.astype(f32)
            return carry

        lax.fori_loop(0, depth, classify, 0, unroll=8)

    table = table_ref[...]
    lane = lax.broadcasted_iota(jnp.int32, table.shape, 1)
    row = lax.broadcasted_iota(jnp.int32, table.shape, 0)
    factor = -3.0 / depth_total * math.log2(math.e)
    table = jnp.where(lax.rem(row, 4) == 3, table * factor, table)
    step = jnp.where(lane == bins - 1, 0.0, pltpu.roll(table, bins - 1, 1) - table)
    tab_ref[0] = table
    tab_ref[1] = step

    for p in range(rows // SUB):

        def view_body(v, carry):
            forward = sign_ref[v] == 0
            start = jnp.where(forward, 0, depth_total - 1)
            stride = jnp.where(forward, 1, -1)
            values = [
                jnp.broadcast_to(tab_ref[0, pl.ds(v * 4 + c, 1), :], (SUB, bins)) for c in range(4)
            ]
            steps = [
                jnp.broadcast_to(tab_ref[1, pl.ds(v * 4 + c, 1), :], (SUB, bins)) for c in range(4)
            ]

            def march(i, state):
                light, total, red, green, blue = state
                x = start + stride * i
                low = low_ref[x, pl.ds(p * SUB, SUB), :]
                frac = frac_ref[x, pl.ds(p * SUB, SUB), :]

                def look(c):
                    return lookup(values[c], low) + frac * lookup(steps[c], low)

                exponent = look(3)
                through = jnp.exp2(exponent)
                weight = light * (1.0 - through)
                return (
                    light * through,
                    total + exponent,
                    red + weight * look(0),
                    green + weight * look(1),
                    blue + weight * look(2),
                )

            zero = jnp.zeros((SUB, cols), f32)
            _, total, red, green, blue = lax.fori_loop(
                0, depth_total, march, (jnp.ones((SUB, cols), f32), zero, zero, zero, zero), unroll=MARCH_UNROLL
            )
            for c, value in enumerate((red, green, blue, 1.0 - jnp.exp2(total))):
                out_ref[v, c, pl.ds(p * SUB, SUB), :] = value
            return carry

        lax.fori_loop(0, views, view_body, 0)


def assemble_kernel(nx, *refs):
    pieces, out, sem = refs[:nx], refs[nx], refs[nx + 1]
    rows = pieces[0].shape[2]
    me = lax.axis_index("gx")
    copies = []
    for k in range(nx):
        at = pl.multiple_of(jnp.bitwise_xor(me, k) * rows, SUB)
        copies.append(pltpu.make_async_copy(pieces[k], out.at[:, :, pl.ds(at, rows), :], sem.at[k]))
        copies[-1].start()
    for copy in copies:
        copy.wait()


def on_device(velocity, view_sign, transfer):
    comps, depth, rows, cols = velocity.shape
    views, channels, bins = transfer.shape
    sizes = tuple(lax.axis_size(a) for a in AXES)
    nx = sizes[0]
    assert all(n & (n - 1) == 0 for n in sizes)
    assert cols == LANES and bins == LANES and rows % (SUB * nx) == 0
    assert depth * (rows // SUB) % LANES == 0
    cell_count = depth * rows * cols * math.prod(sizes)
    counts = tuple(min(n - 1, 2) for n in sizes)
    groups = depth * (rows // SUB) // LANES
    tile = jax.ShapeDtypeStruct((SUB, LANES), f32)
    x_face = jax.ShapeDtypeStruct((comps, rows, cols), f32)
    y_face = jax.ShapeDtypeStruct((comps, depth, cols), f32)
    y_sent = jax.ShapeDtypeStruct((comps + 1, depth, cols), f32)
    z_face = jax.ShapeDtypeStruct((groups * comps + 1, SUB, LANES), f32)
    shapes = [x_face] * counts[0] + [y_face] * counts[1] + [z_face] * counts[2] + [tile]
    *faces, squares = pl.pallas_call(
        functools.partial(faces_kernel, sizes, counts),
        out_shape=shapes,
        in_specs=[ANY],
        out_specs=[VMEM] * len(shapes),
        scratch_shapes=[
            pltpu.VMEM((comps, depth, rows, cols), f32),
            pltpu.SemaphoreType.DMA((CHUNKS,)),
        ],
        compiler_params=limit(4),
        name="faces",
    )(velocity)

    def exchange(sent, axis):
        kinds = (functools.partial(swap, bit_mask=1), swap_across)
        return [kind(x, axis) for x, kind in zip(sent, kinds)]

    def everyone(x, axis):
        for bit in range(lax.axis_size(axis).bit_length() - 1):
            x = x + swap(x, axis, 1 << bit)
        return x

    x_faces, y_faces, z_faces = (
        faces[: counts[0]],
        faces[counts[0] : counts[0] + counts[1]],
        faces[counts[0] + counts[1] :],
    )
    z_halos = exchange(z_faces, "gz")
    x_halos = exchange(x_faces, "gx")
    if sizes[2] == 2:
        tiles = [squares, z_halos[0][groups * comps]]
    else:
        tiles = [everyone(squares, "gz")]
    *y_sents, column = pl.pallas_call(
        functools.partial(attach_kernel, len(y_faces), len(tiles)),
        out_shape=[y_sent] * len(y_faces) + [tile],
        in_specs=[VMEM] * (len(y_faces) + len(tiles)),
        out_specs=[VMEM] * (len(y_faces) + 1),
        compiler_params=limit(2),
        name="attach",
    )(*y_faces, *tiles)
    y_halos = exchange(y_sents, "gy")
    if sizes[1] == 4:
        attached, extra = 2, [column, swap(column, "gy", 2)]
    elif sizes[1] <= 2:
        attached, extra = counts[1], [column]
    else:
        attached, extra = 0, [everyone(column, "gy")]
    part_rows = rows // nx
    piece = jax.ShapeDtypeStruct((depth + 1, part_rows, cols), f32)
    halos = x_halos + y_halos + z_halos
    q_pieces = pl.pallas_call(
        functools.partial(q_kernel, sizes, counts, attached, len(extra)),
        out_shape=[piece] * nx,
        in_specs=[ANY] + [VMEM] * (len(halos) + len(extra)),
        out_specs=[VMEM] * nx,
        scratch_shapes=[
            pltpu.VMEM((comps, depth + 2, rows + 2 * SUB, cols), f32),
            pltpu.SemaphoreType.DMA((1,)),
        ],
        compiler_params=limit(8),
        name="q",
    )(velocity, *halos, *extra)
    order = sorted(range(1, nx), key=lambda k: -k)
    got = {0: q_pieces[0]}
    for k in order:
        got[k] = swap(q_pieces[k], "gx", k)
    image_piece = pl.pallas_call(
        functools.partial(render_kernel, nx, cell_count),
        out_shape=jax.ShapeDtypeStruct((views, channels, part_rows, cols), f32),
        in_specs=[VMEM] * nx + [SMEM, VMEM],
        out_specs=VMEM,
        scratch_shapes=[
            pltpu.VMEM((depth * nx, part_rows, cols), jnp.int32),
            pltpu.VMEM((depth * nx, part_rows, cols), f32),
            pltpu.VMEM((2, views * channels, bins), f32),
        ],
        compiler_params=limit(8),
        name="render",
    )(*[got[k] for k in range(nx)], view_sign, transfer.reshape(views * channels, bins))
    images = {0: image_piece}
    for k in order:
        images[k] = swap(image_piece, "gx", k)
    return pl.pallas_call(
        functools.partial(assemble_kernel, nx),
        out_shape=jax.ShapeDtypeStruct((views, channels, rows, cols), f32),
        in_specs=[VMEM] * nx,
        out_specs=ANY,
        scratch_shapes=[pltpu.SemaphoreType.DMA((nx,))],
        compiler_params=limit(2),
        name="assemble",
    )(*[images[k] for k in range(nx)])


def solution(mesh):
    in_specs = (P(None, "gx", "gy", "gz"), P(), P())
    out_specs = P(None, None, "gy", "gz")
    return jax.shard_map(
        on_device, mesh=mesh, in_specs=in_specs, out_specs=out_specs, check_vma=False
    )
```

```python
import functools
import math

import jax
import jax.numpy as jnp
from jax import lax
from jax.experimental import pallas as pl
from jax.experimental.pallas import tpu as pltpu
from jax.sharding import PartitionSpec as P

SUB, LANES = 8, 128
AXES = ("gx", "gy", "gz")
ANY = pl.BlockSpec(memory_space=pl.ANY)
VMEM = pl.BlockSpec(memory_space=pltpu.VMEM)
SMEM = pl.BlockSpec(memory_space=pltpu.SMEM)
f32 = jnp.float32
EARLY = 48
LATE_UNROLL = 80
CHUNKS = 4
UNITS = 2
PATTERN = (4, 2)


def limit(mib):
    return pltpu.CompilerParams(vmem_limit_bytes=mib * 2**20)


def swap(x, axis, bit_mask):
    n = lax.axis_size(axis)
    return lax.ppermute(x, axis, [(i, i ^ bit_mask) for i in range(n)])


def swap_across(x, axis):
    n = lax.axis_size(axis)
    return lax.ppermute(x, axis, [(i, (i + 1) % n if i % 2 else (i - 1) % n) for i in range(n)])


def flags(sizes):
    out = []
    for axis, n in zip(AXES, sizes):
        i = lax.axis_index(axis)
        out.append((lax.rem(i, 2) == 0, i == 0, i == n - 1))
    return out


def lookup(table, index):
    numbers = lax.GatherDimensionNumbers(
        offset_dims=(),
        collapsed_slice_dims=(1,),
        start_index_map=(1,),
        operand_batching_dims=(0,),
        start_indices_batching_dims=(0,),
    )
    return lax.gather(
        table, index[..., None], numbers, (1, 1), mode=lax.GatherScatterMode.PROMISE_IN_BOUNDS
    )


def faces_kernel(sizes, counts, v_hbm, *refs):
    comps, depth, rows, cols = v_hbm.shape
    tiles = rows // SUB
    info = flags(sizes)
    refs = list(refs)
    x_refs = [refs.pop(0) for _ in range(counts[0])]
    y_refs = [refs.pop(0) for _ in range(counts[1])]
    z_refs = [refs.pop(0) for _ in range(counts[2])]
    sq_ref, v_ref, sem = refs
    chunk = depth // CHUNKS
    copies = []
    for n in range(CHUNKS):
        part = pl.ds(n * chunk, chunk)
        copies.append(pltpu.make_async_copy(v_hbm.at[:, part], v_ref.at[:, part], sem.at[n]))
        copies[-1].start()

    def edge(axis, far, extent):
        at = jnp.where(info[axis][0], extent - 1, 0)
        return extent - 1 - at if far else at

    lane = lax.broadcasted_iota(jnp.int32, (SUB, LANES), 1)
    groups = depth * tiles // LANES
    zero = jnp.zeros((SUB, LANES), f32)
    picked = [[[zero] * comps for _ in range(groups)] for _ in z_refs]
    squares = [zero] * 4
    for n in range(CHUNKS):
        copies[n].wait()
        for x in range(n * chunk, (n + 1) * chunk):
            for far, out in enumerate(y_refs):
                at = edge(1, far, rows)
                for c in range(comps):
                    out[c, pl.ds(x, 1), :] = v_ref[c, x, pl.ds(at, 1), :]
            for c in range(comps):
                for j in range(tiles):
                    tile = v_ref[c, x, pl.ds(j * SUB, SUB), :]
                    squares[j % 4] = squares[j % 4] + tile * tile
                    group, to = divmod(x * tiles + j, LANES)
                    for far in range(len(z_refs)):
                        at = edge(2, far, cols)
                        moved = pltpu.roll(tile, lax.rem(to - at + cols, cols), 1)
                        old = picked[far][group][c]
                        picked[far][group][c] = jnp.where(lane == to, moved, old)
    for far, out in enumerate(x_refs):
        for c in range(comps):
            out[c] = v_ref[c, edge(0, far, depth)]
    total = (squares[0] + squares[1]) + (squares[2] + squares[3])
    sq_ref[...] = total
    for far, out in enumerate(z_refs):
        for g in range(groups):
            for c in range(comps):
                out[g * comps + c] = picked[far][g][c]
        out[groups * comps] = total


def attach_kernel(faces, tiles, *refs):
    face_refs, tile_refs = refs[:faces], refs[faces : faces + tiles]
    outs, sum_ref = refs[faces + tiles : -1], refs[-1]
    total = tile_refs[0][...]
    for t in tile_refs[1:]:
        total = total + t[...]
    sum_ref[...] = total
    for face, out in zip(face_refs, outs):
        comps = face.shape[0]
        out[pl.ds(0, comps)] = face[...]
        out[comps, pl.ds(0, SUB), :] = total


def q_kernel(sizes, counts, attached, extras, v_hbm, *refs):
    comps, depth, rows, cols = v_hbm.shape
    tiles = rows // SUB
    nx = sizes[0]
    refs = list(refs)
    halos = [[refs.pop(0) for _ in range(counts[a])] for a in range(3)]
    extra = [refs.pop(0) for _ in range(extras)]
    outs, (padded, sem) = refs[:nx], refs[nx:]
    info = flags(sizes)
    copy = pltpu.make_async_copy(
        v_hbm, padded.at[:, pl.ds(1, depth), pl.ds(SUB, rows), :], sem.at[0]
    )
    copy.start()

    def both(axis, index):
        even, first, last = info[axis]
        if not halos[axis]:
            return 0.0, 0.0
        near = halos[axis][0][index]
        far = halos[axis][-1][index]
        low = jnp.where(first, 0.0, jnp.where(even, far, near))
        high = jnp.where(last, 0.0, jnp.where(even, near, far))
        return low, high

    for c in range(comps):
        for end, value in zip((0, depth + 1), both(0, c)):
            padded[c, end, pl.ds(SUB, rows), :] = jnp.broadcast_to(value, (rows, cols))
        for end, value in zip((SUB - 1, SUB + rows), both(1, c)):
            value = jnp.broadcast_to(value, (depth, cols))
            for x in range(depth):
                padded[c, 1 + x, pl.ds(end, 1), :] = value[x : x + 1]
    tile_sum = extra[0][...]
    for t in extra[1:]:
        tile_sum = tile_sum + t[...]
    for near_far in halos[1][:attached]:
        tile_sum = tile_sum + near_far[comps, pl.ds(0, SUB), :]
    for out in outs:
        out[depth, pl.ds(0, SUB), :] = tile_sum
    groups = depth * tiles // LANES
    lane = lax.broadcasted_iota(jnp.int32, (SUB, cols), 1)
    me = lax.axis_index("gx")
    piece_tiles = tiles // nx
    per = LANES // tiles
    zeven = info[2][0]
    zero = jnp.zeros((SUB, LANES), f32)
    zhalo = []
    for g in range(groups):
        zhalo.append([])
        for c in range(comps):
            if counts[2] == 1:
                zhalo[g].append(halos[2][0][g * comps + c])
            else:
                zhalo[g].append([zero + h for h in both(2, g * comps + c)])
    copy.wait()
    for k in range(nx):
        for p in range(piece_tiles):
            j = jnp.bitwise_xor(me, k) * piece_tiles + p
            base = j * SUB + SUB
            middle = pl.ds(pl.multiple_of(base, SUB), SUB)
            for x in range(depth):
                g, i = divmod(x, per)
                at = i * tiles + j
                dx, dy, dz = [], [], []
                for c in range(comps):
                    here = padded[c, x + 1, middle, :]
                    dx.append(padded[c, x + 2, middle, :] - padded[c, x, middle, :])
                    dy.append(
                        padded[c, x + 1, pl.ds(base + 1, SUB), :]
                        - padded[c, x + 1, pl.ds(base - 1, SUB), :]
                    )
                    if counts[2] == 1:
                        shift = jnp.where(zeven, cols - 1 - at, lax.rem(cols - at, cols))
                        moved = pltpu.roll(zhalo[g][c], shift, 1)
                        high = jnp.where(zeven, moved, 0.0)
                        low = jnp.where(zeven, 0.0, moved)
                    else:
                        low = pltpu.roll(zhalo[g][c][0], lax.rem(cols - at, cols), 1)
                        high = pltpu.roll(zhalo[g][c][1], cols - 1 - at, 1)
                    up = jnp.where(lane == cols - 1, high, pltpu.roll(here, cols - 1, 1))
                    down = jnp.where(lane == 0, low, pltpu.roll(here, 1, 1))
                    dz.append(up - down)
                cross = dy[0] * dx[1] + dz[0] * dx[2] + dz[1] * dy[2]
                total = dx[0] * dx[0] + dy[1] * dy[1] + dz[2] * dz[2] + (cross + cross)
                outs[k][x, pl.ds(p * SUB, SUB), :] = total


def render_kernel(nx, cell_count, *refs):
    refs = list(refs)
    pieces = [refs.pop(0) for _ in range(nx)]
    sign_ref, table_ref, out_ref, low_ref, lowf_ref, frac_ref, tab_ref, part_ref, late_ref = refs
    planes, rows, cols = pieces[0].shape
    depth = planes - 1
    count, bins = table_ref.shape
    views = count // 4
    depth_total = depth * nx
    me = lax.axis_index("gx")
    squares = pieces[0][depth, pl.ds(0, SUB), :]
    for piece in pieces[1:]:
        squares = squares + piece[depth, pl.ds(0, SUB), :]
    energy = jnp.sum(squares, keepdims=True) / cell_count
    scale = jnp.broadcast_to(-0.25 / (energy + 1e-06), (SUB, cols))
    for k in range(nx):
        base = jnp.bitwise_xor(me, k) * depth

        def classify(x, carry):
            part = pieces[k][x] * scale
            coord = (bins - 1) / (1.0 + jnp.exp(-part))
            low = coord.astype(jnp.int32)
            low_ref[base + x] = low
            lowf_ref[base + x] = low.astype(f32)
            frac_ref[base + x] = coord - low.astype(f32)
            return carry

        lax.fori_loop(0, depth, classify, 0, unroll=8)

    view = lax.broadcasted_iota(jnp.int32, (views, bins), 0)
    lane = lax.broadcasted_iota(jnp.int32, (views, bins), 1)
    side = jnp.zeros((views, bins), f32)
    for v in range(views):
        side = jnp.where(view == v, jnp.where(sign_ref[v] == 0, -1.0, 1.0), side)
    factor = 3.0 / depth_total * math.log2(math.e)
    tables = [table_ref[pl.ds(c, views, stride=4), :] for c in range(4)]
    tables[3] = tables[3] * (side * factor)
    tables += [jnp.where(lane == bins - 1, 0.0, pltpu.roll(t, bins - 1, 1) - t) for t in tables]
    table = jnp.concatenate(tables, axis=0)
    tab_ref[...] = table
    high = table.astype(jnp.bfloat16)
    rest = (table - high.astype(f32)).astype(jnp.bfloat16)
    tall = jnp.concatenate([high, rest], axis=0)
    wide = jnp.concatenate([high, rest], axis=1)
    packed = 2 * SUB
    level = lax.broadcasted_iota(jnp.int32, (packed, cols), 0).astype(f32)
    levels = [(level + float(g * packed)).astype(jnp.bfloat16) for g in range(bins // packed)]
    one = jnp.ones((packed, cols), jnp.bfloat16)
    nil = jnp.zeros((packed, cols), jnp.bfloat16)
    split = EARLY
    steps = (depth_total - split) // LATE_UNROLL
    early_unroll = split // steps
    width = 2

    def advance(state, look):
        total, light, *colour = state
        total = total + look(3)
        after = jnp.exp2(total)
        weight = light - after
        return (total, after, *[old + weight * look(c) for c, old in enumerate(colour)])

    zero = jnp.zeros((SUB, cols), f32)
    start = (zero, jnp.ones((SUB, cols), f32), zero, zero, zero)

    def unit(n, carry):
        spread = [
            jnp.broadcast_to(tab_ref[pl.ds(c * views + n, 1), :], (SUB, bins)) for c in range(8)
        ]

        def march(i, states):
            early, late = states
            for u in range(0, LATE_UNROLL, width):
                columns = []
                for r in range(width):
                    at = lowf_ref[split + i * LATE_UNROLL + u + r, pl.ds(n, 1), :]
                    at = jnp.broadcast_to(at, (packed, cols)).astype(jnp.bfloat16)
                    columns.append(
                        jnp.concatenate([jnp.where(at == l, one, nil) for l in levels], axis=0)
                    )
                chosen = jnp.concatenate(columns, axis=1)
                if u // width % PATTERN[0] < PATTERN[1]:
                    looked = jnp.dot(tall, chosen, preferred_element_type=f32)
                    looked = looked[: 2 * count] + looked[2 * count :]
                else:
                    chosen = jnp.concatenate([chosen, chosen], axis=0)
                    looked = jnp.dot(wide, chosen, preferred_element_type=f32)
                for r in range(width):
                    frac = frac_ref[split + i * LATE_UNROLL + u + r, pl.ds(n, 1), :]
                    frac = jnp.broadcast_to(frac, (views, cols))
                    cells = looked[:, r * cols : (r + 1) * cols]
                    late = advance(
                        late,
                        lambda c: cells[c * views : (c + 1) * views]
                        + frac * cells[count + c * views : count + (c + 1) * views],
                    )
                    first = (u + r) * early_unroll // LATE_UNROLL
                    stop = (u + r + 1) * early_unroll // LATE_UNROLL
                    for e in range(first, stop):
                        x = i * early_unroll + e
                        low = low_ref[x]
                        part = frac_ref[x]
                        early = advance(
                            early,
                            lambda c: lookup(spread[c], low) + part * lookup(spread[4 + c], low),
                        )
            return early, late

        early, late = lax.fori_loop(0, steps, march, (start, start))
        for s, value in enumerate((early[0], *early[2:])):
            part_ref[s, n] = value
        for s, value in enumerate((late[0], *late[2:])):
            late_ref[s, :, pl.ds(n, 1), :] = value[:, None, :]
        return carry

    lax.fori_loop(0, SUB, unit, 0, unroll=UNITS)
    for v in range(views):
        total = part_ref[0, v]
        before = jnp.exp2(total)
        left = jnp.exp2(-jnp.abs(total + late_ref[0, v]))
        turn = jnp.where(sign_ref[v] == 0, 1.0, -left)
        for c in range(3):
            out_ref[v, c] = (part_ref[1 + c, v] + before * late_ref[1 + c, v]) * turn
        out_ref[v, 3] = 1.0 - left


def assemble_kernel(nx, *refs):
    pieces, out, sem = refs[:nx], refs[nx], refs[nx + 1]
    rows = pieces[0].shape[2]
    me = lax.axis_index("gx")
    copies = []
    for k in range(nx):
        at = pl.multiple_of(jnp.bitwise_xor(me, k) * rows, SUB)
        copies.append(pltpu.make_async_copy(pieces[k], out.at[:, :, pl.ds(at, rows), :], sem.at[k]))
        copies[-1].start()
    for copy in copies:
        copy.wait()


def on_device(velocity, view_sign, transfer):
    comps, depth, rows, cols = velocity.shape
    views, channels, bins = transfer.shape
    sizes = tuple(lax.axis_size(a) for a in AXES)
    nx = sizes[0]
    assert all(n & (n - 1) == 0 for n in sizes)
    assert cols == LANES and bins == LANES and rows == SUB * nx and (views, channels) == (SUB, 4)
    assert depth * (rows // SUB) % LANES == 0
    cell_count = depth * rows * cols * math.prod(sizes)
    counts = tuple(min(n - 1, 2) for n in sizes)
    groups = depth * (rows // SUB) // LANES
    tile = jax.ShapeDtypeStruct((SUB, LANES), f32)
    x_face = jax.ShapeDtypeStruct((comps, rows, cols), f32)
    y_face = jax.ShapeDtypeStruct((comps, depth, cols), f32)
    y_sent = jax.ShapeDtypeStruct((comps + 1, depth, cols), f32)
    z_face = jax.ShapeDtypeStruct((groups * comps + 1, SUB, LANES), f32)
    shapes = [x_face] * counts[0] + [y_face] * counts[1] + [z_face] * counts[2] + [tile]
    *faces, squares = pl.pallas_call(
        functools.partial(faces_kernel, sizes, counts),
        out_shape=shapes,
        in_specs=[ANY],
        out_specs=[VMEM] * len(shapes),
        scratch_shapes=[
            pltpu.VMEM((comps, depth, rows, cols), f32),
            pltpu.SemaphoreType.DMA((CHUNKS,)),
        ],
        compiler_params=limit(4),
        name="faces",
    )(velocity)

    def exchange(sent, axis):
        kinds = (functools.partial(swap, bit_mask=1), swap_across)
        return [kind(x, axis) for x, kind in zip(sent, kinds)]

    def everyone(x, axis):
        for bit in range(lax.axis_size(axis).bit_length() - 1):
            x = x + swap(x, axis, 1 << bit)
        return x

    x_faces, y_faces, z_faces = (
        faces[: counts[0]],
        faces[counts[0] : counts[0] + counts[1]],
        faces[counts[0] + counts[1] :],
    )
    z_halos = exchange(z_faces, "gz")
    x_halos = exchange(x_faces, "gx")
    if sizes[2] == 2:
        tiles = [squares, z_halos[0][groups * comps]]
    else:
        tiles = [everyone(squares, "gz")]
    *y_sents, column = pl.pallas_call(
        functools.partial(attach_kernel, len(y_faces), len(tiles)),
        out_shape=[y_sent] * len(y_faces) + [tile],
        in_specs=[VMEM] * (len(y_faces) + len(tiles)),
        out_specs=[VMEM] * (len(y_faces) + 1),
        compiler_params=limit(2),
        name="attach",
    )(*y_faces, *tiles)
    y_halos = exchange(y_sents, "gy")
    if sizes[1] == 4:
        attached, extra = 2, [column, swap(column, "gy", 2)]
    elif sizes[1] <= 2:
        attached, extra = counts[1], [column]
    else:
        attached, extra = 0, [everyone(column, "gy")]
    part_rows = rows // nx
    piece = jax.ShapeDtypeStruct((depth + 1, part_rows, cols), f32)
    halos = x_halos + y_halos + z_halos
    q_pieces = pl.pallas_call(
        functools.partial(q_kernel, sizes, counts, attached, len(extra)),
        out_shape=[piece] * nx,
        in_specs=[ANY] + [VMEM] * (len(halos) + len(extra)),
        out_specs=[VMEM] * nx,
        scratch_shapes=[
            pltpu.VMEM((comps, depth + 2, rows + 2 * SUB, cols), f32),
            pltpu.SemaphoreType.DMA((1,)),
        ],
        compiler_params=limit(8),
        name="q",
    )(velocity, *halos, *extra)
    order = sorted(range(1, nx), key=lambda k: -k)
    got = {0: q_pieces[0]}
    for k in order:
        got[k] = swap(q_pieces[k], "gx", k)
    image_piece = pl.pallas_call(
        functools.partial(render_kernel, nx, cell_count),
        out_shape=jax.ShapeDtypeStruct((views, channels, part_rows, cols), f32),
        in_specs=[VMEM] * nx + [SMEM, VMEM],
        out_specs=VMEM,
        scratch_shapes=[
            pltpu.VMEM((depth * nx, part_rows, cols), jnp.int32),
            pltpu.VMEM((depth * nx, part_rows, cols), f32),
            pltpu.VMEM((depth * nx, part_rows, cols), f32),
            pltpu.VMEM((2 * channels * views, bins), f32),
            pltpu.VMEM((channels, views, part_rows, cols), f32),
            pltpu.VMEM((channels, views, part_rows, cols), f32),
        ],
        compiler_params=limit(8),
        name="render",
    )(*[got[k] for k in range(nx)], view_sign, transfer.reshape(views * channels, bins))
    images = {0: image_piece}
    for k in order:
        images[k] = swap(image_piece, "gx", k)
    return pl.pallas_call(
        functools.partial(assemble_kernel, nx),
        out_shape=jax.ShapeDtypeStruct((views, channels, rows, cols), f32),
        in_specs=[VMEM] * nx,
        out_specs=ANY,
        scratch_shapes=[pltpu.SemaphoreType.DMA((nx,))],
        compiler_params=limit(2),
        name="assemble",
    )(*[images[k] for k in range(nx)])


def solution(mesh):
    in_specs = (P(None, "gx", "gy", "gz"), P(), P())
    out_specs = P(None, None, "gy", "gz")
    return jax.shard_map(
        on_device, mesh=mesh, in_specs=in_specs, out_specs=out_specs, check_vma=False
    )
```

```python
import functools
import math

import jax
import jax.numpy as jnp
from jax import lax
from jax.experimental import pallas as pl
from jax.experimental.pallas import tpu as pltpu
from jax.sharding import PartitionSpec as P

SUB, LANES = 8, 128
AXES = ("gx", "gy", "gz")
ANY = pl.BlockSpec(memory_space=pl.ANY)
VMEM = pl.BlockSpec(memory_space=pltpu.VMEM)
SMEM = pl.BlockSpec(memory_space=pltpu.SMEM)
f32 = jnp.float32
EARLY = 12
CHUNKS = 4
UNITS = 8


def limit(mib):
    return pltpu.CompilerParams(vmem_limit_bytes=mib * 2**20)


def swap(x, axis, bit_mask):
    n = lax.axis_size(axis)
    return lax.ppermute(x, axis, [(i, i ^ bit_mask) for i in range(n)])


def swap_across(x, axis):
    n = lax.axis_size(axis)
    return lax.ppermute(x, axis, [(i, (i + 1) % n if i % 2 else (i - 1) % n) for i in range(n)])


def flags(sizes):
    out = []
    for axis, n in zip(AXES, sizes):
        i = lax.axis_index(axis)
        out.append((lax.rem(i, 2) == 0, i == 0, i == n - 1))
    return out


def lookup(table, index):
    numbers = lax.GatherDimensionNumbers(
        offset_dims=(),
        collapsed_slice_dims=(1,),
        start_index_map=(1,),
        operand_batching_dims=(0,),
        start_indices_batching_dims=(0,),
    )
    return lax.gather(
        table, index[..., None], numbers, (1, 1), mode=lax.GatherScatterMode.PROMISE_IN_BOUNDS
    )


def faces_kernel(sizes, counts, v_hbm, *refs):
    comps, depth, rows, cols = v_hbm.shape
    tiles = rows // SUB
    info = flags(sizes)
    refs = list(refs)
    x_refs = [refs.pop(0) for _ in range(counts[0])]
    y_refs = [refs.pop(0) for _ in range(counts[1])]
    z_refs = [refs.pop(0) for _ in range(counts[2])]
    sq_ref, v_ref, sem = refs
    chunk = depth // CHUNKS
    copies = []
    for n in range(CHUNKS):
        part = pl.ds(n * chunk, chunk)
        copies.append(pltpu.make_async_copy(v_hbm.at[:, part], v_ref.at[:, part], sem.at[n]))
        copies[-1].start()

    def edge(axis, far, extent):
        at = jnp.where(info[axis][0], extent - 1, 0)
        return extent - 1 - at if far else at

    lane = lax.broadcasted_iota(jnp.int32, (SUB, LANES), 1)
    groups = depth * tiles // LANES
    zero = jnp.zeros((SUB, LANES), f32)
    picked = [[[zero] * comps for _ in range(groups)] for _ in z_refs]
    squares = [zero] * 4
    for n in range(CHUNKS):
        copies[n].wait()
        for x in range(n * chunk, (n + 1) * chunk):
            for far, out in enumerate(y_refs):
                at = edge(1, far, rows)
                for c in range(comps):
                    out[c, pl.ds(x, 1), :] = v_ref[c, x, pl.ds(at, 1), :]
            for c in range(comps):
                for j in range(tiles):
                    tile = v_ref[c, x, pl.ds(j * SUB, SUB), :]
                    squares[j % 4] = squares[j % 4] + tile * tile
                    group, to = divmod(x * tiles + j, LANES)
                    for far in range(len(z_refs)):
                        at = edge(2, far, cols)
                        moved = pltpu.roll(tile, lax.rem(to - at + cols, cols), 1)
                        old = picked[far][group][c]
                        picked[far][group][c] = jnp.where(lane == to, moved, old)
    for far, out in enumerate(x_refs):
        for c in range(comps):
            out[c] = v_ref[c, edge(0, far, depth)]
    total = (squares[0] + squares[1]) + (squares[2] + squares[3])
    sq_ref[...] = total
    for far, out in enumerate(z_refs):
        for g in range(groups):
            for c in range(comps):
                out[g * comps + c] = picked[far][g][c]
        out[groups * comps] = total


def attach_kernel(faces, tiles, *refs):
    face_refs, tile_refs = refs[:faces], refs[faces : faces + tiles]
    outs, sum_ref = refs[faces + tiles : -1], refs[-1]
    total = tile_refs[0][...]
    for t in tile_refs[1:]:
        total = total + t[...]
    sum_ref[...] = total
    for face, out in zip(face_refs, outs):
        comps = face.shape[0]
        out[pl.ds(0, comps)] = face[...]
        out[comps, pl.ds(0, SUB), :] = total


def q_kernel(sizes, counts, v_hbm, *refs):
    comps, depth, rows, cols = v_hbm.shape
    tiles = rows // SUB
    nx = sizes[0]
    refs = list(refs)
    halos = [[refs.pop(0) for _ in range(counts[a])] for a in range(3)]
    outs, (padded, sem) = refs[:nx], refs[nx:]
    info = flags(sizes)
    copy = pltpu.make_async_copy(
        v_hbm, padded.at[:, pl.ds(1, depth), pl.ds(SUB, rows), :], sem.at[0]
    )
    copy.start()

    def both(axis, index):
        even, first, last = info[axis]
        if not halos[axis]:
            return 0.0, 0.0
        near = halos[axis][0][index]
        far = halos[axis][-1][index]
        low = jnp.where(first, 0.0, jnp.where(even, far, near))
        high = jnp.where(last, 0.0, jnp.where(even, near, far))
        return low, high

    for c in range(comps):
        for end, value in zip((0, depth + 1), both(0, c)):
            padded[c, end, pl.ds(SUB, rows), :] = jnp.broadcast_to(value, (rows, cols))
        for end, value in zip((SUB - 1, SUB + rows), both(1, c)):
            value = jnp.broadcast_to(value, (depth, cols))
            for x in range(depth):
                padded[c, 1 + x, pl.ds(end, 1), :] = value[x : x + 1]
    groups = depth * tiles // LANES
    lane = lax.broadcasted_iota(jnp.int32, (SUB, cols), 1)
    me = lax.axis_index("gx")
    piece_tiles = tiles // nx
    per = LANES // tiles
    zeven = info[2][0]
    zero = jnp.zeros((SUB, LANES), f32)
    zhalo = []
    for g in range(groups):
        zhalo.append([])
        for c in range(comps):
            if counts[2] == 1:
                zhalo[g].append(halos[2][0][g * comps + c])
            else:
                zhalo[g].append([zero + h for h in both(2, g * comps + c)])
    copy.wait()
    for k in range(nx):
        for p in range(piece_tiles):
            j = jnp.bitwise_xor(me, k) * piece_tiles + p
            base = j * SUB + SUB
            middle = pl.ds(pl.multiple_of(base, SUB), SUB)
            for x in range(depth):
                g, i = divmod(x, per)
                at = i * tiles + j
                dx, dy, dz = [], [], []
                for c in range(comps):
                    here = padded[c, x + 1, middle, :]
                    dx.append(padded[c, x + 2, middle, :] - padded[c, x, middle, :])
                    dy.append(
                        padded[c, x + 1, pl.ds(base + 1, SUB), :]
                        - padded[c, x + 1, pl.ds(base - 1, SUB), :]
                    )
                    if counts[2] == 1:
                        shift = jnp.where(zeven, cols - 1 - at, lax.rem(cols - at, cols))
                        moved = pltpu.roll(zhalo[g][c], shift, 1)
                        high = jnp.where(zeven, moved, 0.0)
                        low = jnp.where(zeven, 0.0, moved)
                    else:
                        low = pltpu.roll(zhalo[g][c][0], lax.rem(cols - at, cols), 1)
                        high = pltpu.roll(zhalo[g][c][1], cols - 1 - at, 1)
                    up = jnp.where(lane == cols - 1, high, pltpu.roll(here, cols - 1, 1))
                    down = jnp.where(lane == 0, low, pltpu.roll(here, 1, 1))
                    dz.append(up - down)
                cross = dy[0] * dx[1] + dz[0] * dx[2] + dz[1] * dy[2]
                total = dx[0] * dx[0] + dy[1] * dy[1] + dz[2] * dz[2] + (cross + cross)
                outs[k][x, pl.ds(p * SUB, SUB), :] = total


def column_kernel(attached, *refs):
    faces, tiles, out = refs[:attached], refs[attached:-1], refs[-1]
    total = tiles[0][...]
    for t in tiles[1:]:
        total = total + t[...]
    for face in faces:
        total = total + face[face.shape[0] - 1, pl.ds(0, SUB), :]
    out[...] = total


def seal_kernel(tiles, *refs):
    total = refs[1][...]
    for t in refs[2 : 1 + tiles]:
        total = total + t[...]
    out, sum_ref = refs[1 + tiles :]
    out[out.shape[0] - 1, pl.ds(0, SUB), :] = total
    sum_ref[...] = total


def render_kernel(nx, cell_count, slabs, carried, earlier, *refs):
    refs = list(refs)
    pieces = [refs.pop(0) for _ in slabs]
    scalers = refs.pop(0)
    states = [refs.pop(0) for _ in earlier]
    sign_ref, table_ref = refs.pop(0), refs.pop(0)
    last = len(slabs) + sum(len(e) for e in earlier) == nx
    out_ref = refs.pop(0)
    scale_ref = refs.pop(0) if carried else None
    low_ref, lowf_ref, frac_ref, tab_ref, part_ref, late_ref = refs
    _, rows, cols = pieces[0].shape
    depth = low_ref.shape[0] // len(slabs)
    count, bins = table_ref.shape
    views = count // 4
    depth_total = depth * nx
    if carried:
        squares = scalers[...]
        if nx > 1:
            squares = squares + pieces[-1][depth, pl.ds(0, SUB), :]
        energy = jnp.sum(squares, keepdims=True) / cell_count
        scale = jnp.broadcast_to(-0.25 / (energy + 1e-06), (SUB, cols))
        scale_ref[...] = scale
    else:
        scale = scalers[...]
    for p, piece in enumerate(pieces):

        def classify(x, carry):
            part = piece[x] * scale
            coord = (bins - 1) / (1.0 + jnp.exp(-part))
            low = coord.astype(jnp.int32)
            low_ref[p * depth + x] = low
            lowf_ref[p * depth + x] = low.astype(f32)
            frac_ref[p * depth + x] = coord - low.astype(f32)
            return carry

        lax.fori_loop(0, depth, classify, 0, unroll=16)

    view = lax.broadcasted_iota(jnp.int32, (views, bins), 0)
    lane = lax.broadcasted_iota(jnp.int32, (views, bins), 1)
    side = jnp.zeros((views, bins), f32)
    for v in range(views):
        side = jnp.where(view == v, jnp.where(sign_ref[v] == 0, -1.0, 1.0), side)
    factor = 3.0 / depth_total * math.log2(math.e)
    tables = [table_ref[pl.ds(c, views, stride=4), :] for c in range(4)]
    tables[3] = tables[3] * (side * factor)
    tables += [jnp.where(lane == bins - 1, 0.0, pltpu.roll(t, bins - 1, 1) - t) for t in tables]
    table = jnp.concatenate(tables, axis=0)
    tab_ref[...] = table
    high = table.astype(jnp.bfloat16)
    rest = (table - high.astype(f32)).astype(jnp.bfloat16)
    tall = jnp.concatenate([high, rest], axis=0)
    wide = jnp.concatenate([high, rest], axis=1)
    packed = 2 * SUB
    level = lax.broadcasted_iota(jnp.int32, (packed, cols), 0).astype(f32)
    levels = [(level + float(g * packed)).astype(jnp.bfloat16) for g in range(bins // packed)]
    one = jnp.ones((packed, cols), jnp.bfloat16)
    nil = jnp.zeros((packed, cols), jnp.bfloat16)
    width = 2
    early_steps = depth * EARLY // 32
    late_steps = depth - early_steps

    def advance(state, look):
        total, light, *colour = state
        total = total + look(3)
        after = jnp.exp2(total)
        weight = light - after
        return (total, after, *[old + weight * look(c) for c, old in enumerate(colour)])

    zero = jnp.zeros((SUB, cols), f32)
    start = (zero, jnp.ones((SUB, cols), f32), zero, zero, zero)

    def unit(t, carry):
        p, n = t // SUB, lax.rem(t, SUB)
        base = p * depth
        spread = [
            jnp.broadcast_to(tab_ref[pl.ds(c * views + n, 1), :], (SUB, bins)) for c in range(8)
        ]
        early = late = start
        done = 0
        for u in range(0, late_steps, width):
            columns = []
            for r in range(width):
                at = lowf_ref[base + early_steps + u + r, pl.ds(n, 1), :]
                at = jnp.broadcast_to(at, (packed, cols)).astype(jnp.bfloat16)
                columns.append(
                    jnp.concatenate([jnp.where(at == l, one, nil) for l in levels], axis=0)
                )
            chosen = jnp.concatenate(columns, axis=1)
            if u // width % 4 < 2:
                looked = jnp.dot(tall, chosen, preferred_element_type=f32)
                looked = looked[: 2 * count] + looked[2 * count :]
            else:
                chosen = jnp.concatenate([chosen, chosen], axis=0)
                looked = jnp.dot(wide, chosen, preferred_element_type=f32)
            for r in range(width):
                frac = frac_ref[base + early_steps + u + r, pl.ds(n, 1), :]
                frac = jnp.broadcast_to(frac, (views, cols))
                cells = looked[:, r * cols : (r + 1) * cols]
                late = advance(
                    late,
                    lambda c: cells[c * views : (c + 1) * views]
                    + frac * cells[count + c * views : count + (c + 1) * views],
                )
                stop = (u + r + 1) * early_steps // late_steps
                while done < stop:
                    low = low_ref[base + done]
                    part = frac_ref[base + done]
                    early = advance(
                        early,
                        lambda c: lookup(spread[c], low) + part * lookup(spread[4 + c], low),
                    )
                    done += 1
        for s, value in enumerate((early[0], *early[2:])):
            part_ref[p, s, n] = value
        for s, value in enumerate((late[0], *late[2:])):
            late_ref[p, s, :, pl.ds(n, 1), :] = value[:, None, :]
        return carry

    lax.fori_loop(0, len(slabs) * SUB, unit, 0, unroll=UNITS)

    def merged(p, v):
        total = part_ref[p, 0, v]
        before = jnp.exp2(total)
        return [total + late_ref[p, 0, v]] + [
            part_ref[p, s, v] + before * late_ref[p, s, v] for s in (1, 2, 3)
        ]

    if not last:
        for p in range(len(slabs)):
            for v in range(views):
                for s, value in enumerate(merged(p, v)):
                    out_ref[p, s, v] = value
        return
    me = lax.axis_index("gx")
    names = [k for e in earlier for k in e] + list(slabs)
    place = [jnp.bitwise_xor(me, k) for k in names]
    ahead = [[jnp.where(place[j] < place[i], 1.0, 0.0) for j in range(nx)] for i in range(nx)]
    for v in range(views):
        rays = [[st[p, s, v] for s in range(4)] for st, e in zip(states, earlier) for p in range(len(e))]
        rays += [merged(p, v) for p in range(len(slabs))]
        total = sum(ray[0] for ray in rays)
        colour = [zero] * 3
        for i in range(nx):
            before = zero
            for j in range(nx):
                if j != i:
                    before = before + ahead[i][j] * rays[j][0]
            before = jnp.exp2(before)
            colour = [old + before * rays[i][1 + c] for c, old in enumerate(colour)]
        left = jnp.exp2(-jnp.abs(total))
        turn = jnp.where(sign_ref[v] == 0, 1.0, -left)
        for c in range(3):
            out_ref[v, c] = colour[c] * turn
        out_ref[v, 3] = 1.0 - left


def assemble_kernel(nx, *refs):
    pieces, out, sem = refs[:nx], refs[nx], refs[nx + 1]
    rows = pieces[0].shape[2]
    me = lax.axis_index("gx")
    copies = []
    for k in range(nx):
        at = pl.multiple_of(jnp.bitwise_xor(me, k) * rows, SUB)
        copies.append(pltpu.make_async_copy(pieces[k], out.at[:, :, pl.ds(at, rows), :], sem.at[k]))
        copies[-1].start()
    for copy in copies:
        copy.wait()


def on_device(velocity, view_sign, transfer):
    comps, depth, rows, cols = velocity.shape
    views, channels, bins = transfer.shape
    sizes = tuple(lax.axis_size(a) for a in AXES)
    nx = sizes[0]
    assert all(n & (n - 1) == 0 for n in sizes)
    assert cols == LANES and bins == LANES and rows == SUB * nx and (views, channels) == (SUB, 4)
    assert depth * (rows // SUB) % LANES == 0
    cell_count = depth * rows * cols * math.prod(sizes)
    counts = tuple(min(n - 1, 2) for n in sizes)
    groups = depth * (rows // SUB) // LANES
    tile = jax.ShapeDtypeStruct((SUB, LANES), f32)
    x_face = jax.ShapeDtypeStruct((comps, rows, cols), f32)
    y_face = jax.ShapeDtypeStruct((comps, depth, cols), f32)
    y_sent = jax.ShapeDtypeStruct((comps + 1, depth, cols), f32)
    z_face = jax.ShapeDtypeStruct((groups * comps + 1, SUB, LANES), f32)
    shapes = [x_face] * counts[0] + [y_face] * counts[1] + [z_face] * counts[2] + [tile]
    *faces, squares = pl.pallas_call(
        functools.partial(faces_kernel, sizes, counts),
        out_shape=shapes,
        in_specs=[ANY],
        out_specs=[VMEM] * len(shapes),
        scratch_shapes=[
            pltpu.VMEM((comps, depth, rows, cols), f32),
            pltpu.SemaphoreType.DMA((CHUNKS,)),
        ],
        compiler_params=limit(4),
        name="faces",
    )(velocity)

    def exchange(sent, axis):
        kinds = (functools.partial(swap, bit_mask=1), swap_across)
        return [kind(x, axis) for x, kind in zip(sent, kinds)]

    def everyone(x, axis):
        for bit in range(lax.axis_size(axis).bit_length() - 1):
            x = x + swap(x, axis, 1 << bit)
        return x

    x_faces, y_faces, z_faces = (
        faces[: counts[0]],
        faces[counts[0] : counts[0] + counts[1]],
        faces[counts[0] + counts[1] :],
    )
    z_halos = exchange(z_faces, "gz")
    x_halos = exchange(x_faces, "gx")
    if sizes[2] == 2:
        tiles = [squares, z_halos[0][groups * comps]]
    else:
        tiles = [everyone(squares, "gz")]
    *y_sents, column = pl.pallas_call(
        functools.partial(attach_kernel, len(y_faces), len(tiles)),
        out_shape=[y_sent] * len(y_faces) + [tile],
        in_specs=[VMEM] * (len(y_faces) + len(tiles)),
        out_specs=[VMEM] * (len(y_faces) + 1),
        compiler_params=limit(2),
        name="attach",
    )(*y_faces, *tiles)
    y_halos = exchange(y_sents, "gy")
    if sizes[1] == 4:
        attached, extra = 2, [column, swap(column, "gy", 2)]
    elif sizes[1] <= 2:
        attached, extra = counts[1], [column]
    else:
        attached, extra = 0, [everyone(column, "gy")]
    column = pl.pallas_call(
        functools.partial(column_kernel, attached),
        out_shape=tile,
        in_specs=[VMEM] * (attached + len(extra)),
        out_specs=VMEM,
        compiler_params=limit(2),
        name="column",
    )(*y_halos[:attached], *extra)
    tiles = [column]
    for bit in range(nx.bit_length() - 2):
        if bit:
            tiles = [tiles[0] + tiles[1]]
        tiles.append(swap(tiles[0], "gx", 1 << bit))
    part_rows = rows // nx
    plain = jax.ShapeDtypeStruct((depth, part_rows, cols), f32)
    sealed = jax.ShapeDtypeStruct((depth + 1, part_rows, cols), f32)
    halos = x_halos + y_halos + z_halos
    q_pieces = pl.pallas_call(
        functools.partial(q_kernel, sizes, counts),
        out_shape=[sealed if k == nx - 1 else plain for k in range(nx)],
        in_specs=[ANY] + [VMEM] * len(halos),
        out_specs=[VMEM] * nx,
        scratch_shapes=[
            pltpu.VMEM((comps, depth + 2, rows + 2 * SUB, cols), f32),
            pltpu.SemaphoreType.DMA((1,)),
        ],
        compiler_params=limit(8),
        name="q",
    )(velocity, *halos)
    *q_pieces, last_piece = q_pieces
    last_piece, squares = pl.pallas_call(
        functools.partial(seal_kernel, len(tiles)),
        out_shape=[sealed, tile],
        in_specs=[VMEM] * (1 + len(tiles)),
        out_specs=[VMEM] * 2,
        input_output_aliases={0: 0},
        compiler_params=limit(2),
        name="seal",
    )(last_piece, *tiles)
    q_pieces = [*q_pieces, last_piece]
    order = sorted(range(1, nx), key=lambda k: -k)
    got = {0: q_pieces[0]}
    for k in order:
        got[k] = swap(q_pieces[k], "gx", k)
    scale, states, earlier = squares, [], []
    table = transfer.reshape(views * channels, bins)
    rays = (channels, views, part_rows, cols)
    for slabs in [[0] + order[:1]] + [[k] for k in order[1:]]:
        carried = not earlier
        last = len(slabs) + sum(len(e) for e in earlier) == nx
        image = jax.ShapeDtypeStruct((views, channels, part_rows, cols), f32)
        shapes = [image if last else jax.ShapeDtypeStruct((len(slabs), *rays), f32)]
        out = pl.pallas_call(
            functools.partial(render_kernel, nx, cell_count, slabs, carried, tuple(earlier)),
            out_shape=shapes + [tile] * carried,
            in_specs=[VMEM] * (len(slabs) + 1 + len(states)) + [SMEM, VMEM],
            out_specs=[VMEM] * (1 + carried),
            scratch_shapes=[
                pltpu.VMEM((depth * len(slabs), part_rows, cols), jnp.int32),
                pltpu.VMEM((depth * len(slabs), part_rows, cols), f32),
                pltpu.VMEM((depth * len(slabs), part_rows, cols), f32),
                pltpu.VMEM((2 * channels * views, bins), f32),
                pltpu.VMEM((len(slabs), *rays), f32),
                pltpu.VMEM((len(slabs), *rays), f32),
            ],
            compiler_params=limit(8),
            name="render",
        )(*[got[k] for k in slabs], scale, *states, view_sign, table)
        if carried:
            scale = out[1]
        states.append(out[0])
        earlier.append(tuple(slabs))
    image_piece = states[-1]
    images = {0: image_piece}
    for k in order:
        images[k] = swap(image_piece, "gx", k)
    return pl.pallas_call(
        functools.partial(assemble_kernel, nx),
        out_shape=jax.ShapeDtypeStruct((views, channels, rows, cols), f32),
        in_specs=[VMEM] * nx,
        out_specs=ANY,
        scratch_shapes=[pltpu.SemaphoreType.DMA((nx,))],
        compiler_params=limit(2),
        name="assemble",
    )(*[images[k] for k in range(nx)])


def solution(mesh):
    in_specs = (P(None, "gx", "gy", "gz"), P(), P())
    out_specs = P(None, None, "gy", "gz")
    return jax.shard_map(
        on_device, mesh=mesh, in_specs=in_specs, out_specs=out_specs, check_vma=False
    )
```

```python
import functools
import math

import jax
import jax.numpy as jnp
from jax import lax
from jax.experimental import pallas as pl
from jax.experimental.pallas import tpu as pltpu
from jax.sharding import PartitionSpec as P

SUB, LANES = 8, 128
AXES = ("gx", "gy", "gz")
ANY = pl.BlockSpec(memory_space=pl.ANY)
HBM = pl.BlockSpec(memory_space=pltpu.HBM)
VMEM = pl.BlockSpec(memory_space=pltpu.VMEM)
SMEM = pl.BlockSpec(memory_space=pltpu.SMEM)
f32 = jnp.float32
EARLY = 48
LATE_UNROLL = 80
UNITS = 2
PATTERN = (4, 2)


def limit(mib):
    return pltpu.CompilerParams(vmem_limit_bytes=mib * 2**20)


def swap(x, axis, bit_mask):
    n = lax.axis_size(axis)
    return lax.ppermute(x, axis, [(i, i ^ bit_mask) for i in range(n)])


def swap_across(x, axis):
    n = lax.axis_size(axis)
    return lax.ppermute(x, axis, [(i, (i + 1) % n if i % 2 else (i - 1) % n) for i in range(n)])


def flags(sizes):
    out = []
    for axis, n in zip(AXES, sizes):
        i = lax.axis_index(axis)
        out.append((lax.rem(i, 2) == 0, i == 0, i == n - 1))
    return out


def lookup(table, index):
    numbers = lax.GatherDimensionNumbers(
        offset_dims=(),
        collapsed_slice_dims=(1,),
        start_index_map=(1,),
        operand_batching_dims=(0,),
        start_indices_batching_dims=(0,),
    )
    return lax.gather(
        table, index[..., None], numbers, (1, 1), mode=lax.GatherScatterMode.PROMISE_IN_BOUNDS
    )


def edge(info, axis, far, extent):
    at = jnp.where(info[axis][0], extent - 1, 0)
    return extent - 1 - at if far else at


def faces_kernel(sizes, counts, v_hbm, *refs):
    comps, depth, rows, cols = v_hbm.shape
    info = flags(sizes)
    x_refs, y_refs = refs[: counts[0]], refs[counts[0] : counts[0] + counts[1]]
    band, sem = refs[counts[0] + counts[1] :]
    copies = []
    for far, out in enumerate(x_refs):
        source = v_hbm.at[:, edge(info, 0, far, depth)]
        copies.append(pltpu.make_async_copy(source, out, sem.at[far]))
    for far in range(len(y_refs)):
        at = pl.multiple_of(edge(info, 1, far, rows) // SUB * SUB, SUB)
        source = v_hbm.at[:, :, pl.ds(at, SUB), :]
        copies.append(pltpu.make_async_copy(source, band.at[far], sem.at[2 + far]))
    for copy in copies:
        copy.start()
    for copy in copies:
        copy.wait()
    for far, out in enumerate(y_refs):
        at = lax.rem(edge(info, 1, far, rows), SUB)
        for c in range(comps):
            for x in range(depth):
                out[c, pl.ds(x, 1), :] = band[far, c, x, pl.ds(at, 1), :]


def ends_kernel(sizes, counts, v_ref, *refs):
    comps, depth, rows, cols = v_ref.shape
    tiles = rows // SUB
    info = flags(sizes)
    z_refs, sq_ref = refs[: counts[2]], refs[counts[2]]
    lane = lax.broadcasted_iota(jnp.int32, (SUB, LANES), 1)
    groups = depth * tiles // LANES
    zero = jnp.zeros((SUB, LANES), f32)
    picked = [[[zero] * comps for _ in range(groups)] for _ in z_refs]
    squares = [zero] * 4
    for x in range(depth):
        for c in range(comps):
            for j in range(tiles):
                tile = v_ref[c, x, pl.ds(j * SUB, SUB), :]
                squares[j % 4] = squares[j % 4] + tile * tile
                group, to = divmod(x * tiles + j, LANES)
                for far in range(len(z_refs)):
                    at = edge(info, 2, far, cols)
                    moved = pltpu.roll(tile, lax.rem(to - at + cols, cols), 1)
                    old = picked[far][group][c]
                    picked[far][group][c] = jnp.where(lane == to, moved, old)
    total = (squares[0] + squares[1]) + (squares[2] + squares[3])
    sq_ref[...] = total
    for far, out in enumerate(z_refs):
        for g in range(groups):
            for c in range(comps):
                out[g * comps + c] = picked[far][g][c]
        out[groups * comps] = total


def column_kernel(*refs):
    *tiles, out = refs
    total = tiles[0][...]
    for t in tiles[1:]:
        total = total + (t[...] if len(t.shape) == 2 else t[t.shape[0] - 1])
    out[...] = total


def seal_kernel(pieces, *refs):
    tiles, outs = refs[pieces:-pieces], refs[-pieces:]
    total = tiles[0][...]
    for t in tiles[1:]:
        total = total + t[...]
    for out in outs:
        out[out.shape[0] - 1, pl.ds(0, SUB), :] = total


def q_kernel(sizes, counts, v_hbm, *refs):
    comps, depth, rows, cols = v_hbm.shape
    tiles = rows // SUB
    nx = sizes[0]
    refs = list(refs)
    halos = [[refs.pop(0) for _ in range(counts[a])] for a in range(3)]
    outs, (padded, sem) = refs[:nx], refs[nx:]
    info = flags(sizes)
    copy = pltpu.make_async_copy(
        v_hbm, padded.at[:, pl.ds(1, depth), pl.ds(SUB, rows), :], sem.at[0]
    )
    copy.start()

    def both(axis, index):
        even, first, last = info[axis]
        if not halos[axis]:
            return 0.0, 0.0
        near = halos[axis][0][index]
        far = halos[axis][-1][index]
        low = jnp.where(first, 0.0, jnp.where(even, far, near))
        high = jnp.where(last, 0.0, jnp.where(even, near, far))
        return low, high

    for c in range(comps):
        for end, value in zip((0, depth + 1), both(0, c)):
            padded[c, end, pl.ds(SUB, rows), :] = jnp.broadcast_to(value, (rows, cols))
        for end, value in zip((SUB - 1, SUB + rows), both(1, c)):
            value = jnp.broadcast_to(value, (depth, cols))
            for x in range(depth):
                padded[c, 1 + x, pl.ds(end, 1), :] = value[x : x + 1]
    groups = depth * tiles // LANES
    lane = lax.broadcasted_iota(jnp.int32, (SUB, cols), 1)
    me = lax.axis_index("gx")
    piece_tiles = tiles // nx
    per = LANES // tiles
    zeven = info[2][0]
    zero = jnp.zeros((SUB, LANES), f32)
    zhalo = []
    for g in range(groups):
        zhalo.append([])
        for c in range(comps):
            if counts[2] == 1:
                zhalo[g].append(halos[2][0][g * comps + c])
            else:
                zhalo[g].append([zero + h for h in both(2, g * comps + c)])
    copy.wait()
    for k in range(nx):
        for p in range(piece_tiles):
            j = jnp.bitwise_xor(me, k) * piece_tiles + p
            base = j * SUB + SUB
            middle = pl.ds(pl.multiple_of(base, SUB), SUB)
            for x in range(depth):
                g, i = divmod(x, per)
                at = i * tiles + j
                dx, dy, dz = [], [], []
                for c in range(comps):
                    here = padded[c, x + 1, middle, :]
                    dx.append(padded[c, x + 2, middle, :] - padded[c, x, middle, :])
                    dy.append(
                        padded[c, x + 1, pl.ds(base + 1, SUB), :]
                        - padded[c, x + 1, pl.ds(base - 1, SUB), :]
                    )
                    if counts[2] == 1:
                        shift = jnp.where(zeven, cols - 1 - at, lax.rem(cols - at, cols))
                        moved = pltpu.roll(zhalo[g][c], shift, 1)
                        high = jnp.where(zeven, moved, 0.0)
                        low = jnp.where(zeven, 0.0, moved)
                    else:
                        low = pltpu.roll(zhalo[g][c][0], lax.rem(cols - at, cols), 1)
                        high = pltpu.roll(zhalo[g][c][1], cols - 1 - at, 1)
                    up = jnp.where(lane == cols - 1, high, pltpu.roll(here, cols - 1, 1))
                    down = jnp.where(lane == 0, low, pltpu.roll(here, 1, 1))
                    dz.append(up - down)
                cross = dy[0] * dx[1] + dz[0] * dx[2] + dz[1] * dy[2]
                total = dx[0] * dx[0] + dy[1] * dy[1] + dz[2] * dz[2] + (cross + cross)
                outs[k][x, pl.ds(p * SUB, SUB), :] = total


def render_kernel(nx, cell_count, *refs):
    refs = list(refs)
    pieces = [refs.pop(0) for _ in range(nx)]
    sign_ref, table_ref, out_ref, low_ref, lowf_ref, frac_ref, tab_ref, part_ref, late_ref = refs
    planes, rows, cols = pieces[0].shape
    depth = planes - 1
    count, bins = table_ref.shape
    views = count // 4
    depth_total = depth * nx
    me = lax.axis_index("gx")
    squares = pieces[0][depth, pl.ds(0, SUB), :]
    for piece in pieces[1:]:
        squares = squares + piece[depth, pl.ds(0, SUB), :]
    energy = jnp.sum(squares, keepdims=True) / cell_count
    scale = jnp.broadcast_to(-0.25 / (energy + 1e-06), (SUB, cols))
    for k in range(nx):
        base = jnp.bitwise_xor(me, k) * depth

        def classify(x, carry):
            part = pieces[k][x] * scale
            coord = (bins - 1) / (1.0 + jnp.exp(-part))
            low = coord.astype(jnp.int32)
            low_ref[base + x] = low
            lowf_ref[base + x] = low.astype(f32)
            frac_ref[base + x] = coord - low.astype(f32)
            return carry

        lax.fori_loop(0, depth, classify, 0, unroll=8)

    view = lax.broadcasted_iota(jnp.int32, (views, bins), 0)
    lane = lax.broadcasted_iota(jnp.int32, (views, bins), 1)
    side = jnp.zeros((views, bins), f32)
    for v in range(views):
        side = jnp.where(view == v, jnp.where(sign_ref[v] == 0, -1.0, 1.0), side)
    factor = 3.0 / depth_total * math.log2(math.e)
    tables = [table_ref[pl.ds(c, views, stride=4), :] for c in range(4)]
    tables[3] = tables[3] * (side * factor)
    tables += [jnp.where(lane == bins - 1, 0.0, pltpu.roll(t, bins - 1, 1) - t) for t in tables]
    table = jnp.concatenate(tables, axis=0)
    tab_ref[...] = table
    high = table.astype(jnp.bfloat16)
    rest = (table - high.astype(f32)).astype(jnp.bfloat16)
    tall = jnp.concatenate([high, rest], axis=0)
    wide = jnp.concatenate([high, rest], axis=1)
    packed = 2 * SUB
    level = lax.broadcasted_iota(jnp.int32, (packed, cols), 0).astype(f32)
    levels = [(level + float(g * packed)).astype(jnp.bfloat16) for g in range(bins // packed)]
    one = jnp.ones((packed, cols), jnp.bfloat16)
    nil = jnp.zeros((packed, cols), jnp.bfloat16)
    split = EARLY
    steps = (depth_total - split) // LATE_UNROLL
    early_unroll = split // steps
    width = 2

    def advance(state, look):
        total, light, *colour = state
        total = total + look(3)
        after = jnp.exp2(total)
        weight = light - after
        return (total, after, *[old + weight * look(c) for c, old in enumerate(colour)])

    zero = jnp.zeros((SUB, cols), f32)
    start = (zero, jnp.ones((SUB, cols), f32), zero, zero, zero)

    def unit(n, carry):
        spread = [
            jnp.broadcast_to(tab_ref[pl.ds(c * views + n, 1), :], (SUB, bins)) for c in range(8)
        ]

        def march(i, states):
            early, late = states
            for u in range(0, LATE_UNROLL, width):
                columns = []
                for r in range(width):
                    at = lowf_ref[split + i * LATE_UNROLL + u + r, pl.ds(n, 1), :]
                    at = jnp.broadcast_to(at, (packed, cols)).astype(jnp.bfloat16)
                    columns.append(
                        jnp.concatenate([jnp.where(at == l, one, nil) for l in levels], axis=0)
                    )
                chosen = jnp.concatenate(columns, axis=1)
                if u // width % PATTERN[0] < PATTERN[1]:
                    looked = jnp.dot(tall, chosen, preferred_element_type=f32)
                    looked = looked[: 2 * count] + looked[2 * count :]
                else:
                    chosen = jnp.concatenate([chosen, chosen], axis=0)
                    looked = jnp.dot(wide, chosen, preferred_element_type=f32)
                for r in range(width):
                    frac = frac_ref[split + i * LATE_UNROLL + u + r, pl.ds(n, 1), :]
                    frac = jnp.broadcast_to(frac, (views, cols))
                    cells = looked[:, r * cols : (r + 1) * cols]
                    late = advance(
                        late,
                        lambda c: cells[c * views : (c + 1) * views]
                        + frac * cells[count + c * views : count + (c + 1) * views],
                    )
                    first = (u + r) * early_unroll // LATE_UNROLL
                    stop = (u + r + 1) * early_unroll // LATE_UNROLL
                    for e in range(first, stop):
                        x = i * early_unroll + e
                        low = low_ref[x]
                        part = frac_ref[x]
                        early = advance(
                            early,
                            lambda c: lookup(spread[c], low) + part * lookup(spread[4 + c], low),
                        )
            return early, late

        early, late = lax.fori_loop(0, steps, march, (start, start))
        for s, value in enumerate((early[0], *early[2:])):
            part_ref[s, n] = value
        for s, value in enumerate((late[0], *late[2:])):
            late_ref[s, :, pl.ds(n, 1), :] = value[:, None, :]
        return carry

    lax.fori_loop(0, SUB, unit, 0, unroll=UNITS)
    for v in range(views):
        total = part_ref[0, v]
        before = jnp.exp2(total)
        left = jnp.exp2(-jnp.abs(total + late_ref[0, v]))
        turn = jnp.where(sign_ref[v] == 0, 1.0, -left)
        for c in range(3):
            out_ref[v, c] = (part_ref[1 + c, v] + before * late_ref[1 + c, v]) * turn
        out_ref[v, 3] = 1.0 - left


def assemble_kernel(nx, *refs):
    pieces, out, sem = refs[:nx], refs[nx], refs[nx + 1]
    rows = pieces[0].shape[2]
    me = lax.axis_index("gx")
    copies = []
    for k in range(nx):
        at = pl.multiple_of(jnp.bitwise_xor(me, k) * rows, SUB)
        copies.append(pltpu.make_async_copy(pieces[k], out.at[:, :, pl.ds(at, rows), :], sem.at[k]))
        copies[-1].start()
    for copy in copies:
        copy.wait()


def on_device(velocity, view_sign, transfer):
    comps, depth, rows, cols = velocity.shape
    views, channels, bins = transfer.shape
    sizes = tuple(lax.axis_size(a) for a in AXES)
    nx = sizes[0]
    assert all(n & (n - 1) == 0 for n in sizes)
    assert cols == LANES and bins == LANES and rows == SUB * nx and (views, channels) == (SUB, 4)
    assert depth * (rows // SUB) % LANES == 0
    cell_count = depth * rows * cols * math.prod(sizes)
    counts = tuple(min(n - 1, 2) for n in sizes)
    groups = depth * (rows // SUB) // LANES
    tile = jax.ShapeDtypeStruct((SUB, LANES), f32)
    x_face = jax.ShapeDtypeStruct((comps, rows, cols), f32)
    y_face = jax.ShapeDtypeStruct((comps, depth, cols), f32)
    z_face = jax.ShapeDtypeStruct((groups * comps + 1, SUB, LANES), f32)
    faces = pl.pallas_call(
        functools.partial(faces_kernel, sizes, counts),
        out_shape=[x_face] * counts[0] + [y_face] * counts[1],
        in_specs=[HBM],
        out_specs=[VMEM] * (counts[0] + counts[1]),
        scratch_shapes=[
            pltpu.VMEM((2, comps, depth, SUB, cols), f32),
            pltpu.SemaphoreType.DMA((4,)),
        ],
        compiler_params=limit(2),
        name="faces",
    )(pltpu.with_memory_space_constraint(velocity, pltpu.HBM))
    *z_faces, squares = pl.pallas_call(
        functools.partial(ends_kernel, sizes, counts),
        out_shape=[z_face] * counts[2] + [tile],
        in_specs=[VMEM],
        out_specs=[VMEM] * (counts[2] + 1),
        compiler_params=limit(4),
        name="ends",
    )(velocity)

    def exchange(sent, axis):
        kinds = (functools.partial(swap, bit_mask=1), swap_across)
        return [kind(x, axis) for x, kind in zip(sent, kinds)]

    def column(*tiles):
        return pl.pallas_call(
            column_kernel,
            out_shape=tile,
            in_specs=[VMEM] * len(tiles),
            out_specs=VMEM,
            compiler_params=limit(2),
            name="column",
        )(*tiles)

    def others(x, axis):
        n = lax.axis_size(axis)
        while n > 4:
            n //= 2
            x = x + swap(x, axis, n)
        return [x] + [swap(x, axis, k) for k in range(1, n)]

    x_halos = exchange(faces[: counts[0]], "gx")
    y_halos = exchange(faces[counts[0] :], "gy")
    z_halos = exchange(z_faces, "gz")
    tiles = [squares, z_halos[0]] if sizes[2] == 2 else others(squares, "gz")
    tiles = others(column(*tiles), "gy")
    part_rows = rows // nx
    piece = jax.ShapeDtypeStruct((depth + 1, part_rows, cols), f32)
    halos = x_halos + y_halos + z_halos
    q_pieces = pl.pallas_call(
        functools.partial(q_kernel, sizes, counts),
        out_shape=[piece] * nx,
        in_specs=[ANY] + [VMEM] * len(halos),
        out_specs=[VMEM] * nx,
        scratch_shapes=[
            pltpu.VMEM((comps, depth + 2, rows + 2 * SUB, cols), f32),
            pltpu.SemaphoreType.DMA((1,)),
        ],
        compiler_params=limit(8),
        name="q",
    )(velocity, *halos)
    q_pieces = pl.pallas_call(
        functools.partial(seal_kernel, nx),
        out_shape=[piece] * nx,
        in_specs=[VMEM] * (nx + len(tiles)),
        out_specs=[VMEM] * nx,
        input_output_aliases={k: k for k in range(nx)},
        compiler_params=limit(2),
        name="seal",
    )(*q_pieces, *tiles)
    order = sorted(range(1, nx), key=lambda k: -k)
    got = {0: q_pieces[0]}
    for k in order:
        got[k] = swap(q_pieces[k], "gx", k)
    image_piece = pl.pallas_call(
        functools.partial(render_kernel, nx, cell_count),
        out_shape=jax.ShapeDtypeStruct((views, channels, part_rows, cols), f32),
        in_specs=[VMEM] * nx + [SMEM, VMEM],
        out_specs=VMEM,
        scratch_shapes=[
            pltpu.VMEM((depth * nx, part_rows, cols), jnp.int32),
            pltpu.VMEM((depth * nx, part_rows, cols), f32),
            pltpu.VMEM((depth * nx, part_rows, cols), f32),
            pltpu.VMEM((2 * channels * views, bins), f32),
            pltpu.VMEM((channels, views, part_rows, cols), f32),
            pltpu.VMEM((channels, views, part_rows, cols), f32),
        ],
        compiler_params=limit(8),
        name="render",
    )(*[got[k] for k in range(nx)], view_sign, transfer.reshape(views * channels, bins))
    images = {0: image_piece}
    for k in order:
        images[k] = swap(image_piece, "gx", k)
    return pl.pallas_call(
        functools.partial(assemble_kernel, nx),
        out_shape=jax.ShapeDtypeStruct((views, channels, rows, cols), f32),
        in_specs=[VMEM] * nx,
        out_specs=ANY,
        scratch_shapes=[pltpu.SemaphoreType.DMA((nx,))],
        compiler_params=limit(2),
        name="assemble",
    )(*[images[k] for k in range(nx)])


def solution(mesh):
    in_specs = (P(None, "gx", "gy", "gz"), P(), P())
    out_specs = P(None, None, "gy", "gz")
    return jax.shard_map(
        on_device, mesh=mesh, in_specs=in_specs, out_specs=out_specs, check_vma=False
    )
```
